128 devices in a mesh: grp: 8 (over x_hi, y), dom: 16 (over z, x_lo, core).
Axes of the slice: x: 4 (x_hi: 2, x_lo: 2; x = x_hi * 2 + x_lo), y: 4, z: 4, core: 2. Of those that a mesh axis runs over, the one named last changes fastest.
Arguments:
- features: bfloat16 [65536, 1024], P(('grp', 'dom')), may hold values from -6 to 6
- node_order: int32 [65536], P(('grp', 'dom')), may hold values from 0 to 65535, as said below
- block_cols: int32 [512, 16], P(('grp', 'dom')), may hold values from 0 to 63
- block_count: int32 [512], P(('grp', 'dom')), may hold values from 1 to 16, as said below
- block_vals: bfloat16 [512, 16, 128, 128], P(('grp', 'dom')), may hold values from -0.1875 to 0.1875
- weight: bfloat16 [1024, 512], replicated, may hold values from -0.1875 to 0.1875
- cotangent: bfloat16 [65536, 512], P(('grp', 'dom')), may hold values from -12 to 12
Outputs:
- hidden: bfloat16 [65536, 512], P(('grp', 'dom'))
- grad_weight: float32 [1024, 512], replicated
The draws below stay inside these ranges and needn't reach their ends.
Inputs may be any that keep to these rules, and one draw needn't show every extreme that they name: `node_order`: A permutation of the crawl rows; the positions of one device's block of 512 take exactly 4 crawl rows from each device's block of 512 crawl rows. `block_count`: some row of blocks holds exactly 16 live blocks.
All inputs are finite; a program needn't handle non-finite values.
Results may differ from the reference program's by a relative error of at most 0.014.
Values may be sent and summed in bfloat16 or wider, within the bound.
A program may use at most 128 MiB of HBM per device.

```python
import jax
import jax.numpy as jnp
from jax import lax

F = 1024
H = 512
TILE = 128
BLOCKS = 16
ROWS_DEV = 512
GROUP_TILES = 64
N_NODES = 65536
TILES = 512
N_GRP = 8
N_DOM = 16


def draw_node_order(key, part):
    key = jax.random.fold_in(key, 71)
    devices = N_GRP * N_DOM
    pair_rows = ROWS_DEV // devices
    key_src, key_dst = jax.random.split(key)
    source = jax.vmap(lambda subkey: jax.random.permutation(subkey, ROWS_DEV))(jax.random.split(key_src, devices)).astype(jnp.int32)
    target = jax.vmap(lambda subkey: jax.random.permutation(subkey, ROWS_DEV))(jax.random.split(key_dst, devices)).astype(jnp.int32)
    offsets = (jnp.arange(devices, dtype=jnp.int32) * ROWS_DEV)[:, None, None]
    values = (source.reshape(devices, devices, pair_rows) + offsets).transpose(1, 0, 2).reshape(devices, ROWS_DEV)
    result = jnp.zeros((devices, ROWS_DEV), jnp.int32).at[jnp.arange(devices, dtype=jnp.int32)[:, None], target].set(values)
    return result.reshape(-1)


def draw_block_count(key, part):
    key = jax.random.fold_in(key, 72)
    devices = N_GRP * N_DOM
    tiles_dev = ROWS_DEV // TILE
    key_cap, key_count, key_busy = jax.random.split(key, 3)
    capacity = jax.random.randint(key_cap, (devices,), BLOCKS // 4, BLOCKS + 1).astype(jnp.int32)
    busiest = jax.random.randint(key_busy, (), 0, devices).astype(jnp.int32)
    capacity = capacity.at[busiest].set(BLOCKS)
    counts = jax.random.randint(key_count, (devices, tiles_dev), 1, capacity[:, None] + 1).astype(jnp.int32)
    counts = counts.at[busiest, 0].set(BLOCKS)
    return counts.reshape(-1)


def draw_cotangent(key, part):
    key = jax.random.fold_in(key, 73)
    key_main = jax.random.fold_in(key, 0)
    position = jnp.arange(N_NODES, dtype=jnp.float32) / N_NODES
    row_scale = (3.0 ** position)[:, None]
    values = jnp.clip(jax.random.normal(key_main, (N_NODES, H), jnp.float32), -4.0, 4.0) * row_scale
    return values.astype(jnp.bfloat16)


def plant(values, rng, least, top_value):
    place = [jax.random.randint(jax.random.fold_in(rng, axis), (), 0, length) for axis, length in enumerate(values.shape)]
    longest = values.shape.index(max(values.shape))
    next_to = place[:longest] + [(place[longest] + 1) % values.shape[longest]] + place[longest + 1:]
    return values.at[tuple(place)].set(least).at[tuple(next_to)].set(top_value)


def level_of(key, dims, pieces, least, top_value):
    loudness, own = 1.0, jax.random.fold_in(key, 6)
    for dim, blocks in pieces:
        heights = jnp.exp(jax.random.uniform(jax.random.fold_in(own, dim), (blocks,), jnp.float32, least / len(pieces), top_value / len(pieces)))
        loudness = loudness * jnp.repeat(heights, dims[dim] // blocks).reshape([-1 if axis == dim else 1 for axis in range(len(dims))])
    return loudness


def gaussian(rng, extent, scale, bound, cuts=(), held_as=jnp.bfloat16):
    values = scale * jax.random.normal(rng, extent, jnp.float32)
    if cuts:
        values = values * level_of(rng, extent, cuts, -0.22, 0.18)
    return jnp.clip(values, -bound, bound).astype(held_as)


def setup_inputs(seed: int = 0) -> dict:
    streams_of = jax.random.split(jax.random.key(seed), 8)
    features = gaussian(streams_of[0], (N_NODES, F), 1.0, 6.0, ((0, 128),))
    node_order = draw_node_order(jax.random.fold_in(streams_of[7], 71), 0)
    block_cols = plant(jax.random.randint(streams_of[2], (TILES, BLOCKS), 0, GROUP_TILES), jax.random.fold_in(streams_of[2], 1), 0, GROUP_TILES - 1).astype(jnp.int32)
    block_count = draw_block_count(jax.random.fold_in(streams_of[7], 71), 0)
    block_vals = gaussian(streams_of[4], (TILES, BLOCKS, TILE, TILE), (TILE * BLOCKS // 2) ** -0.5, 0.1875, ((0, 128),))
    weight = gaussian(streams_of[5], (F, H), F ** -0.5, 0.1875)
    cotangent = draw_cotangent(jax.random.fold_in(streams_of[7], 71), 0)
    return dict(features=features, node_order=node_order, block_cols=block_cols, block_count=block_count, block_vals=block_vals, weight=weight, cotangent=cotangent)


def silu_slope(values):
    sig = jax.nn.sigmoid(values)
    return sig * (1.0 + values * (1.0 - sig))


def reference(features, node_order, block_cols, block_count, block_vals, weight, cotangent):
    ordered = features[node_order]
    transformed = jnp.dot(ordered, weight, preferred_element_type=jnp.float32).astype(jnp.bfloat16)
    tiles_dev = ROWS_DEV // TILE
    z_tiles = transformed.reshape(N_GRP, GROUP_TILES, TILE, H)
    cols_all = block_cols.reshape(N_GRP, N_DOM, tiles_dev, BLOCKS)
    live_all = (jnp.arange(BLOCKS, dtype=jnp.int32)[None, :] < block_count[:, None]).reshape(N_GRP, N_DOM, tiles_dev, BLOCKS)
    vals_all = block_vals.reshape(N_GRP, N_DOM, tiles_dev, BLOCKS, TILE, TILE)
    cot_all = cotangent.reshape(N_GRP, N_DOM, tiles_dev, TILE, H)

    def group_pass(inputs):
        gathered, cols_grp, live_grp, vals_grp, cot_grp = inputs

        def device_forward(dev_in):
            cols_dev, live_dev, vals_dev = dev_in
            masked_vals = jnp.where(live_dev[:, :, None, None], vals_dev.astype(jnp.float32), 0.0)
            selected = gathered[cols_dev].astype(jnp.float32)
            return jnp.einsum('tkij,tkjh->tih', masked_vals, selected)

        aggregate = lax.map(device_forward, (cols_grp, live_grp, vals_grp))
        hidden_grp = jax.nn.silu(aggregate).astype(jnp.bfloat16)
        grad_agg = (cot_grp.astype(jnp.float32) * silu_slope(aggregate)).astype(jnp.bfloat16)

        def device_backward(carry, dev_in):
            cols_dev, live_dev, vals_dev, grad_dev = dev_in
            masked_vals = jnp.where(live_dev[:, :, None, None], vals_dev.astype(jnp.float32), 0.0)
            contrib = jnp.einsum('tkij,tih->tkjh', masked_vals, grad_dev.astype(jnp.float32))
            partial_value = jnp.zeros((GROUP_TILES, TILE, H), jnp.float32).at[cols_dev.reshape(-1)].add(contrib.reshape(-1, TILE, H))
            partial_value = lax.optimization_barrier(partial_value.astype(jnp.bfloat16)).astype(jnp.float32)
            return carry + partial_value, None

        summed, unused = lax.scan(device_backward, jnp.zeros((GROUP_TILES, TILE, H), jnp.float32),
                                  (cols_grp, live_grp, vals_grp, grad_agg))
        return hidden_grp, summed

    hidden_all, grad_rows = lax.map(group_pass, (z_tiles, cols_all, live_all, vals_all, cot_all))
    hidden = hidden_all.reshape(N_NODES, H)
    grad_transformed = grad_rows.reshape(N_NODES, H)
    grad_weight = jnp.dot(ordered.astype(jnp.float32).T, grad_transformed, precision=lax.Precision.HIGHEST)
    return hidden, grad_weight
```

```python
import jax
import jax.numpy as jnp
from jax import lax
from jax.sharding import PartitionSpec as P


def silu_slope(values):
    sig = jax.nn.sigmoid(values)
    return sig * (1.0 + values * (1.0 - sig))


def regroup(features, node_order):
    row_count, width_in = features.shape
    devices = lax.axis_size("grp") * lax.axis_size("dom")
    per_pair = row_count // devices
    source_device = node_order // row_count
    source_row = node_order % row_count
    ordering = jnp.argsort(source_device, stable=True)
    requests = source_row[ordering].reshape(devices, per_pair)
    asked_rows = lax.all_to_all(requests, ("grp", "dom"), split_axis=0, concat_axis=0, tiled=True)
    outgoing = features[asked_rows.reshape(-1)].reshape(devices, per_pair, width_in)
    arrived = lax.all_to_all(outgoing, ("grp", "dom"), split_axis=0, concat_axis=0, tiled=True)
    arrived = arrived.reshape(row_count, width_in)
    inverse = jnp.argsort(ordering)
    return arrived[inverse]


def shards(features, node_order, block_cols, block_count, block_vals, weight, cotangent):
    row_count, width_in = features.shape
    hidden_units = weight.shape[1]
    tiles_dev, blocks, tile_size, _ = block_vals.shape
    ordered = regroup(features, node_order)
    everyone = lax.all_gather(ordered, "dom", axis=0, tiled=True)
    panel_tiles = everyone.reshape(-1, tile_size, width_in)
    live_mask = lax.broadcasted_iota(jnp.int32, (tiles_dev, blocks), 1) < block_count[:, None]
    masked_vals = jnp.where(live_mask[:, :, None, None], block_vals, jnp.zeros((), jnp.bfloat16))
    selected = panel_tiles[block_cols]
    mixed = jnp.einsum("tkij,tkjf->tif", masked_vals, selected, preferred_element_type=jnp.float32)
    mixed = mixed.astype(jnp.bfloat16).reshape(row_count, width_in)
    aggregate = jnp.dot(mixed, weight, preferred_element_type=jnp.float32)
    hidden = jax.nn.silu(aggregate).astype(jnp.bfloat16)
    grad_agg = (cotangent.astype(jnp.float32) * silu_slope(aggregate)).astype(jnp.bfloat16)
    local_grad = lax.dot_general(
        mixed, grad_agg, (((0,), (0,)), ((), ())), preferred_element_type=jnp.float32
    )
    grad_weight = lax.psum(local_grad, ("grp", "dom"))
    return (hidden, grad_weight)


def solution(mesh):
    placed = (
        P(("grp", "dom"), None),
        P(("grp", "dom")),
        P(("grp", "dom"), None),
        P(("grp", "dom")),
        P(("grp", "dom"), None, None, None),
        P(),
        P(("grp", "dom"), None),
    )
    return jax.shard_map(
        shards,
        mesh=mesh,
        in_specs=placed,
        out_specs=(P(("grp", "dom"), None), P()),
        check_vma=False,
    )
```

```python
import jax
import jax.numpy as jnp
from jax import lax
from jax.experimental import pallas as pl
from jax.experimental.pallas import tpu as pltpu
from jax.sharding import PartitionSpec as P

AXES = ("grp", "dom")


def regroup(features, node_order):
    row_count, width_in = features.shape
    devices = lax.axis_size("grp") * lax.axis_size("dom")
    per_pair = row_count // devices
    source_device = node_order // row_count
    source_row = node_order % row_count
    ordering = jnp.argsort(source_device, stable=True)
    requests = source_row[ordering].reshape(devices, per_pair)
    asked_rows = lax.all_to_all(requests, AXES, split_axis=0, concat_axis=0, tiled=True)
    outgoing = features[asked_rows.reshape(-1)].reshape(devices, per_pair, width_in)
    arrived = lax.all_to_all(outgoing, AXES, split_axis=0, concat_axis=0, tiled=True)
    arrived = arrived.reshape(row_count, width_in)
    inverse = jnp.argsort(ordering)
    return arrived[inverse]


def local_kernel(cols, count, panel, vals, weight, cot, hidden, term, chosen, acc, mixed, sems):
    tiles, blocks, size, _ = vals.shape

    def fetch(t, k):
        return pltpu.make_async_copy(panel.at[cols[t, k]], chosen.at[t, k], sems.at[t, k])

    for t in range(tiles):
        @pl.loop(0, count[t])
        def _(k):
            fetch(t, k).start()

    for t in range(tiles):
        live = count[t]
        fetch(t, 0).wait()
        acc[...] = jnp.dot(vals[t, 0], chosen[t, 0], preferred_element_type=jnp.float32)

        @pl.loop(1, live)
        def _(k):
            fetch(t, k).wait()
            acc[...] += jnp.dot(vals[t, k], chosen[t, k], preferred_element_type=jnp.float32)

        mixed[pl.ds(t * size, size), :] = acc[...].astype(jnp.bfloat16)

    rows = mixed[...]
    aggregate = jnp.dot(rows, weight[...], preferred_element_type=jnp.float32)
    sig = jax.nn.sigmoid(aggregate)
    hidden[...] = (aggregate * sig).astype(hidden.dtype)
    slope = sig * (1.0 + aggregate * (1.0 - sig))
    grad_agg = (cot[...].astype(jnp.float32) * slope).astype(jnp.bfloat16)
    term[...] = lax.dot_general(
        rows, grad_agg, (((0,), (0,)), ((), ())), preferred_element_type=jnp.float32
    ).astype(term.dtype)


def local_pass(everyone, block_cols, block_count, block_vals, weight, cotangent):
    tiles, blocks, size, _ = block_vals.shape
    rows, hidden_units = cotangent.shape
    width_in = weight.shape[0]
    panel = everyone.reshape(-1, size, width_in)
    vmem = pl.BlockSpec(memory_space=pltpu.VMEM)
    smem = pl.BlockSpec(memory_space=pltpu.SMEM)
    return pl.pallas_call(
        local_kernel,
        out_shape=(
            jax.ShapeDtypeStruct((rows, hidden_units), jnp.bfloat16),
            jax.ShapeDtypeStruct((width_in, hidden_units), jnp.bfloat16),
        ),
        in_specs=[smem, smem, pl.BlockSpec(memory_space=pl.ANY), vmem, vmem, vmem],
        out_specs=(vmem, vmem),
        scratch_shapes=[
            pltpu.VMEM((tiles, blocks, size, width_in), jnp.bfloat16),
            pltpu.VMEM((size, width_in), jnp.float32),
            pltpu.VMEM((rows, width_in), jnp.bfloat16),
            pltpu.SemaphoreType.DMA((tiles, blocks)),
        ],
        name="local_pass",
    )(block_cols, block_count, panel, block_vals, weight, cotangent)


def sum_terms(term):
    devices = lax.axis_size("grp") * lax.axis_size("dom")
    width_in, hidden_units = term.shape
    share = width_in // devices
    pieces = lax.all_to_all(
        term.reshape(devices, share, hidden_units), AXES, split_axis=0, concat_axis=0, tiled=True
    )
    summed = jnp.sum(pieces.astype(jnp.float32), axis=0).astype(jnp.bfloat16)
    copies = jnp.broadcast_to(summed[None], (devices, share, hidden_units))
    whole = lax.all_to_all(copies, AXES, split_axis=0, concat_axis=0, tiled=True)
    return whole.reshape(width_in, hidden_units).astype(jnp.float32)


def shards(features, node_order, block_cols, block_count, block_vals, weight, cotangent):
    ordered = regroup(features, node_order)
    everyone = lax.all_gather(ordered, "dom", axis=0, tiled=True)
    hidden, term = local_pass(everyone, block_cols, block_count, block_vals, weight, cotangent)
    return (hidden, sum_terms(term))


def solution(mesh):
    placed = (
        P(AXES, None),
        P(AXES),
        P(AXES, None),
        P(AXES),
        P(AXES, None, None, None),
        P(),
        P(AXES, None),
    )
    return jax.shard_map(
        shards,
        mesh=mesh,
        in_specs=placed,
        out_specs=(P(AXES, None), P()),
        check_vma=False,
    )
```

```python
import jax
import jax.numpy as jnp
from jax import lax
from jax.experimental import pallas as pl
from jax.experimental.pallas import tpu as pltpu
from jax.sharding import PartitionSpec as P

AXES = ("grp", "dom")


def regroup(features, node_order):
    row_count, width_in = features.shape
    devices = lax.axis_size("grp") * lax.axis_size("dom")
    per_pair = row_count // devices
    source_device = node_order // row_count
    source_row = node_order % row_count
    ordering = jnp.argsort(source_device, stable=True)
    requests = source_row[ordering].reshape(devices, per_pair)
    asked_rows = lax.all_to_all(requests, AXES, split_axis=0, concat_axis=0, tiled=True)
    outgoing = features[asked_rows.reshape(-1)].reshape(devices, per_pair, width_in)
    arrived = lax.all_to_all(outgoing, AXES, split_axis=0, concat_axis=0, tiled=True)
    arrived = arrived.reshape(row_count, width_in)
    inverse = jnp.argsort(ordering)
    return arrived[inverse]


def piece_plan(rows):
    half = rows // 2
    cut = rows * 11 // 32
    upper = rows - cut
    up = [
        (0, -1, 0, half, None), (0, -1, half, rows, None), (0, 2, 0, half, ("up", 0)),
        (1, -1, 0, cut, ("side", 0)), (1, 2, cut, half, ("side", 2)), (1, 2, 0, cut, ("up", 3)),
    ]
    down = [
        (0, 1, half, rows, None), (0, 1, 0, half, None), (0, 2, half, rows, ("down", 0)),
        (1, 1, upper, rows, ("side", 1)), (1, 2, half, upper, ("side", 3)), (1, 2, upper, rows, ("down", 3)),
    ]
    side = [
        (1, 0, 0, half, None), (1, 0, half, rows, None), (1, -1, cut, half, ("up", 0)),
        (1, 1, half, upper, ("down", 0)), (1, -1, half, rows, ("up", 1)), (1, 1, 0, half, ("down", 1)),
    ]
    return {"up": up, "down": down, "side": side}


ARRIVALS = (
    ("up", 0), ("down", 0), ("side", 0), ("up", 1), ("down", 1), ("side", 1), ("side", 2), ("side", 3),
    ("up", 2), ("down", 2), ("side", 4), ("up", 3), ("down", 3), ("up", 4), ("down", 4), ("side", 5),
    ("up", 5), ("down", 5),
)
LINKS = ("up", "down", "side")


def gather_kernel(own, out, send_sems, recv_sems, pass_send, pass_recv, keep_sem):
    rows = own.shape[0]
    me = lax.axis_index("dom")
    depth, column, core = me // 4, (me // 2) % 2, me % 2

    def place(other_column, shift, which_core):
        z = lax.rem(depth + shift + 4, 4)
        x = column + other_column * (1 - 2 * column)
        return z * 4 + x * 2 + which_core

    partner = place(0, 0, 1 - core)
    targets = {"up": place(0, 1, core), "down": place(0, -1, core), "side": place(1, 0, core)}

    barrier = pltpu.get_barrier_semaphore()
    for target in (*targets.values(), partner):
        pl.semaphore_signal(barrier, inc=1, device_id={"dom": target}, device_id_type=pl.DeviceIdType.MESH)
    keep = pltpu.make_async_copy(own, out.at[me], keep_sem)
    keep.start()
    pl.semaphore_wait(barrier, 4)

    plan = piece_plan(rows)
    moved = {"up": (0, 1), "down": (0, -1), "side": (1, 0)}

    def send(link, number):
        other, shift, low, high, _ = plan[link][number]
        jump, step = moved[link]
        span = pl.ds(low, high - low)
        source_other, source_shift = (other + jump) % 2, shift + step
        owner = place(source_other, source_shift, core)
        slot = LINKS.index(link) * 6 + number
        block = own.at[span] if plan[link][number][4] is None else out.at[owner, span]
        return pltpu.make_async_remote_copy(
            src_ref=block, dst_ref=out.at[owner, span],
            send_sem=send_sems.at[slot], recv_sem=recv_sems.at[slot],
            device_id={"dom": targets[link]}, device_id_type=pl.DeviceIdType.MESH,
        )

    def landed(link, number):
        other, shift, low, high, _ = plan[link][number]
        span = pl.ds(low, high - low)
        slot = LINKS.index(link) * 6 + number
        here = out.at[place(other, shift, core), span]
        return pltpu.make_async_remote_copy(
            src_ref=here, dst_ref=here,
            send_sem=send_sems.at[slot], recv_sem=recv_sems.at[slot],
            device_id={"dom": targets[link]}, device_id_type=pl.DeviceIdType.MESH,
        )

    def hand_over(number, block, there):
        return pltpu.make_async_remote_copy(
            src_ref=block, dst_ref=there,
            send_sem=pass_send.at[number], recv_sem=pass_recv.at[number],
            device_id={"dom": partner}, device_id_type=pl.DeviceIdType.MESH,
        )

    sent = []
    for number in range(2):
        for link in LINKS:
            copy = send(link, number)
            copy.start()
            sent.append(copy)
    copy = hand_over(18, own, out.at[me])
    copy.start()
    sent.append(copy)

    for order, (link, number) in enumerate(ARRIVALS):
        landed(link, number).wait_recv()
        for onward in LINKS:
            for later in range(2, 6):
                if plan[onward][later][4] == (link, number):
                    copy = send(onward, later)
                    copy.start()
                    sent.append(copy)
        other, shift, low, high, _ = plan[link][number]
        here = out.at[place(other, shift, core), pl.ds(low, high - low)]
        copy = hand_over(order, here, here)
        copy.start()
        sent.append(copy)

    hand_over(18, own, out.at[partner]).wait_recv()
    for order, (link, number) in enumerate(ARRIVALS):
        other, shift, low, high, _ = plan[link][number]
        there = out.at[place(other, shift, 1 - core), pl.ds(low, high - low)]
        hand_over(order, there, there).wait_recv()
    for copy in sent:
        copy.wait_send()
    keep.wait()


def gather_group(ordered):
    rows, width_in = ordered.shape
    group = lax.axis_size("dom")
    return pl.pallas_call(
        gather_kernel,
        out_shape=jax.ShapeDtypeStruct((group, rows, width_in), ordered.dtype),
        in_specs=[pl.BlockSpec(memory_space=pltpu.VMEM)],
        out_specs=pl.BlockSpec(memory_space=pl.ANY),
        scratch_shapes=[
            pltpu.SemaphoreType.DMA((18,)),
            pltpu.SemaphoreType.DMA((18,)),
            pltpu.SemaphoreType.DMA((19,)),
            pltpu.SemaphoreType.DMA((19,)),
            pltpu.SemaphoreType.DMA,
        ],
        compiler_params=pltpu.CompilerParams(collective_id=0, has_side_effects=True),
        name="gather_group",
    )(ordered)


def local_kernel(cols, count, panel, vals, weight, cot, hidden, term, chosen, acc, mixed, sems):
    tiles, blocks, size, _ = vals.shape

    def fetch(t, k):
        return pltpu.make_async_copy(panel.at[cols[t, k]], chosen.at[t, k], sems.at[t, k])

    for t in range(tiles):
        @pl.loop(0, count[t])
        def _(k):
            fetch(t, k).start()

    for t in range(tiles):
        live = count[t]
        fetch(t, 0).wait()
        acc[...] = jnp.dot(vals[t, 0], chosen[t, 0], preferred_element_type=jnp.float32)

        @pl.loop(1, live)
        def _(k):
            fetch(t, k).wait()
            acc[...] += jnp.dot(vals[t, k], chosen[t, k], preferred_element_type=jnp.float32)

        mixed[pl.ds(t * size, size), :] = acc[...].astype(jnp.bfloat16)

    rows = mixed[...]
    aggregate = jnp.dot(rows, weight[...], preferred_element_type=jnp.float32)
    sig = jax.nn.sigmoid(aggregate)
    hidden[...] = (aggregate * sig).astype(hidden.dtype)
    slope = sig * (1.0 + aggregate * (1.0 - sig))
    grad_agg = (cot[...].astype(jnp.float32) * slope).astype(jnp.bfloat16)
    term[...] = lax.dot_general(
        rows, grad_agg, (((0,), (0,)), ((), ())), preferred_element_type=jnp.float32
    ).astype(term.dtype)


def local_pass(everyone, block_cols, block_count, block_vals, weight, cotangent):
    tiles, blocks, size, _ = block_vals.shape
    rows, hidden_units = cotangent.shape
    width_in = weight.shape[0]
    panel = everyone.reshape(-1, size, width_in)
    vmem = pl.BlockSpec(memory_space=pltpu.VMEM)
    smem = pl.BlockSpec(memory_space=pltpu.SMEM)
    return pl.pallas_call(
        local_kernel,
        out_shape=(
            jax.ShapeDtypeStruct((rows, hidden_units), jnp.bfloat16),
            jax.ShapeDtypeStruct((width_in, hidden_units), jnp.bfloat16),
        ),
        in_specs=[smem, smem, pl.BlockSpec(memory_space=pl.ANY), vmem, vmem, vmem],
        out_specs=(vmem, vmem),
        scratch_shapes=[
            pltpu.VMEM((tiles, blocks, size, width_in), jnp.bfloat16),
            pltpu.VMEM((size, width_in), jnp.float32),
            pltpu.VMEM((rows, width_in), jnp.bfloat16),
            pltpu.SemaphoreType.DMA((tiles, blocks)),
        ],
        name="local_pass",
    )(block_cols, block_count, panel, block_vals, weight, cotangent)


def sum_terms(term):
    devices = lax.axis_size("grp") * lax.axis_size("dom")
    width_in, hidden_units = term.shape
    share = width_in // devices
    pieces = lax.all_to_all(
        term.reshape(devices, share, hidden_units), AXES, split_axis=0, concat_axis=0, tiled=True
    )
    summed = jnp.sum(pieces.astype(jnp.float32), axis=0).astype(jnp.bfloat16)
    copies = jnp.broadcast_to(summed[None], (devices, share, hidden_units))
    whole = lax.all_to_all(copies, AXES, split_axis=0, concat_axis=0, tiled=True)
    return whole.reshape(width_in, hidden_units).astype(jnp.float32)


def shards(features, node_order, block_cols, block_count, block_vals, weight, cotangent):
    ordered = regroup(features, node_order)
    everyone = gather_group(ordered)
    hidden, term = local_pass(everyone, block_cols, block_count, block_vals, weight, cotangent)
    return (hidden, sum_terms(term))


def solution(mesh):
    placed = (
        P(AXES, None),
        P(AXES),
        P(AXES, None),
        P(AXES),
        P(AXES, None, None, None),
        P(),
        P(AXES, None),
    )
    return jax.shard_map(
        shards,
        mesh=mesh,
        in_specs=placed,
        out_specs=(P(AXES, None), P()),
        check_vma=False,
    )
```

```python
import jax
import jax.numpy as jnp
from jax import lax
from jax.experimental import pallas as pl
from jax.experimental.pallas import tpu as pltpu
from jax.sharding import PartitionSpec as P

AXES = ("grp", "dom")


def regroup(features, node_order):
    row_count, width_in = features.shape
    devices = lax.axis_size("grp") * lax.axis_size("dom")
    per_pair = row_count // devices
    source_device = node_order // row_count
    source_row = node_order % row_count
    ordering = jnp.argsort(source_device, stable=True)
    requests = source_row[ordering].reshape(devices, per_pair)
    asked_rows = lax.all_to_all(requests, AXES, split_axis=0, concat_axis=0, tiled=True)
    outgoing = features[asked_rows.reshape(-1)].reshape(devices, per_pair, width_in)
    arrived = lax.all_to_all(outgoing, AXES, split_axis=0, concat_axis=0, tiled=True)
    arrived = arrived.reshape(row_count, width_in)
    inverse = jnp.argsort(ordering)
    return arrived[inverse]


def piece_plan(rows):
    half = rows // 2
    cut = rows * 11 // 32
    upper = rows - cut
    up = [
        (0, -1, 0, half, None), (0, -1, half, rows, None), (0, 2, 0, half, ("up", 0)),
        (1, -1, 0, cut, ("side", 0)), (1, 2, cut, half, ("side", 2)), (1, 2, 0, cut, ("up", 3)),
    ]
    down = [
        (0, 1, half, rows, None), (0, 1, 0, half, None), (0, 2, half, rows, ("down", 0)),
        (1, 1, upper, rows, ("side", 1)), (1, 2, half, upper, ("side", 3)), (1, 2, upper, rows, ("down", 3)),
    ]
    side = [
        (1, 0, 0, half, None), (1, 0, half, rows, None), (1, -1, cut, half, ("up", 0)),
        (1, 1, half, upper, ("down", 0)), (1, -1, half, rows, ("up", 1)), (1, 1, 0, half, ("down", 1)),
    ]
    return {"up": up, "down": down, "side": side}


ARRIVALS = (
    ("up", 0), ("down", 0), ("side", 0), ("up", 1), ("down", 1), ("side", 1), ("side", 2), ("side", 3),
    ("up", 2), ("down", 2), ("side", 4), ("up", 3), ("down", 3), ("up", 4), ("down", 4), ("side", 5),
    ("up", 5), ("down", 5),
)
LINKS = ("up", "down", "side")


def gather_kernel(own, out, send_sems, recv_sems, pass_send, pass_recv, keep_sem):
    rows = own.shape[0]
    me = lax.axis_index("dom")
    depth, column, core = me // 4, (me // 2) % 2, me % 2

    def place(other_column, shift, which_core):
        z = lax.rem(depth + shift + 4, 4)
        x = column + other_column * (1 - 2 * column)
        return z * 4 + x * 2 + which_core

    partner = place(0, 0, 1 - core)
    targets = {"up": place(0, 1, core), "down": place(0, -1, core), "side": place(1, 0, core)}

    barrier = pltpu.get_barrier_semaphore()
    for target in (*targets.values(), partner):
        pl.semaphore_signal(barrier, inc=1, device_id={"dom": target}, device_id_type=pl.DeviceIdType.MESH)
    keep = pltpu.make_async_copy(own, out.at[me], keep_sem)
    keep.start()
    pl.semaphore_wait(barrier, 4)

    plan = piece_plan(rows)
    moved = {"up": (0, 1), "down": (0, -1), "side": (1, 0)}

    def send(link, number):
        other, shift, low, high, _ = plan[link][number]
        jump, step = moved[link]
        span = pl.ds(low, high - low)
        source_other, source_shift = (other + jump) % 2, shift + step
        owner = place(source_other, source_shift, core)
        slot = LINKS.index(link) * 6 + number
        block = own.at[span] if plan[link][number][4] is None else out.at[owner, span]
        return pltpu.make_async_remote_copy(
            src_ref=block, dst_ref=out.at[owner, span],
            send_sem=send_sems.at[slot], recv_sem=recv_sems.at[slot],
            device_id={"dom": targets[link]}, device_id_type=pl.DeviceIdType.MESH,
        )

    def landed(link, number):
        other, shift, low, high, _ = plan[link][number]
        span = pl.ds(low, high - low)
        slot = LINKS.index(link) * 6 + number
        here = out.at[place(other, shift, core), span]
        return pltpu.make_async_remote_copy(
            src_ref=here, dst_ref=here,
            send_sem=send_sems.at[slot], recv_sem=recv_sems.at[slot],
            device_id={"dom": targets[link]}, device_id_type=pl.DeviceIdType.MESH,
        )

    def hand_over(number, block, there):
        return pltpu.make_async_remote_copy(
            src_ref=block, dst_ref=there,
            send_sem=pass_send.at[number], recv_sem=pass_recv.at[number],
            device_id={"dom": partner}, device_id_type=pl.DeviceIdType.MESH,
        )

    sent = []
    for number in range(2):
        for link in LINKS:
            copy = send(link, number)
            copy.start()
            sent.append(copy)
    copy = hand_over(18, own, out.at[me])
    copy.start()
    sent.append(copy)

    for order, (link, number) in enumerate(ARRIVALS):
        landed(link, number).wait_recv()
        for onward in LINKS:
            for later in range(2, 6):
                if plan[onward][later][4] == (link, number):
                    copy = send(onward, later)
                    copy.start()
                    sent.append(copy)
        other, shift, low, high, _ = plan[link][number]
        here = out.at[place(other, shift, core), pl.ds(low, high - low)]
        copy = hand_over(order, here, here)
        copy.start()
        sent.append(copy)

    hand_over(18, own, out.at[partner]).wait_recv()
    for order, (link, number) in enumerate(ARRIVALS):
        other, shift, low, high, _ = plan[link][number]
        there = out.at[place(other, shift, 1 - core), pl.ds(low, high - low)]
        hand_over(order, there, there).wait_recv()
    for copy in sent:
        copy.wait_send()
    keep.wait()


def gather_group(ordered):
    rows, width_in = ordered.shape
    group = lax.axis_size("dom")
    return pl.pallas_call(
        gather_kernel,
        out_shape=jax.ShapeDtypeStruct((group, rows, width_in), ordered.dtype),
        in_specs=[pl.BlockSpec(memory_space=pltpu.VMEM)],
        out_specs=pl.BlockSpec(memory_space=pl.ANY),
        scratch_shapes=[
            pltpu.SemaphoreType.DMA((18,)),
            pltpu.SemaphoreType.DMA((18,)),
            pltpu.SemaphoreType.DMA((19,)),
            pltpu.SemaphoreType.DMA((19,)),
            pltpu.SemaphoreType.DMA,
        ],
        compiler_params=pltpu.CompilerParams(collective_id=0, has_side_effects=True),
        name="gather_group",
    )(ordered)


def local_kernel(cols, count, panel, vals, weight, cot, hidden, term, chosen, acc, mixed, sems):
    tiles, blocks, size, _ = vals.shape

    def fetch(t, k):
        return pltpu.make_async_copy(panel.at[cols[t, k]], chosen.at[t, k], sems.at[t, k])

    for t in range(tiles):
        @pl.loop(0, count[t])
        def _(k):
            fetch(t, k).start()

    for t in range(tiles):
        live = count[t]
        fetch(t, 0).wait()
        acc[...] = jnp.dot(vals[t, 0], chosen[t, 0], preferred_element_type=jnp.float32)

        @pl.loop(1, live)
        def _(k):
            fetch(t, k).wait()
            acc[...] += jnp.dot(vals[t, k], chosen[t, k], preferred_element_type=jnp.float32)

        mixed[pl.ds(t * size, size), :] = acc[...].astype(jnp.bfloat16)

    rows = mixed[...]
    aggregate = jnp.dot(rows, weight[...], preferred_element_type=jnp.float32)
    sig = jax.nn.sigmoid(aggregate)
    hidden[...] = (aggregate * sig).astype(hidden.dtype)
    slope = sig * (1.0 + aggregate * (1.0 - sig))
    grad_agg = (cot[...].astype(jnp.float32) * slope).astype(jnp.bfloat16)
    products = lax.dot_general(
        rows, grad_agg, (((0,), (0,)), ((), ())), preferred_element_type=jnp.float32
    ).astype(term.dtype)
    columns = term.shape[2]
    for side in range(2):
        term[side] = products[:, side * columns:(side + 1) * columns]


def local_pass(everyone, block_cols, block_count, block_vals, weight, cotangent):
    tiles, blocks, size, _ = block_vals.shape
    rows, hidden_units = cotangent.shape
    width_in = weight.shape[0]
    panel = everyone.reshape(-1, size, width_in)
    vmem = pl.BlockSpec(memory_space=pltpu.VMEM)
    smem = pl.BlockSpec(memory_space=pltpu.SMEM)
    return pl.pallas_call(
        local_kernel,
        out_shape=(
            jax.ShapeDtypeStruct((rows, hidden_units), jnp.bfloat16),
            jax.ShapeDtypeStruct((2, width_in, hidden_units // 2), jnp.bfloat16),
        ),
        in_specs=[smem, smem, pl.BlockSpec(memory_space=pl.ANY), vmem, vmem, vmem],
        out_specs=(vmem, vmem),
        scratch_shapes=[
            pltpu.VMEM((tiles, blocks, size, width_in), jnp.bfloat16),
            pltpu.VMEM((size, width_in), jnp.float32),
            pltpu.VMEM((rows, width_in), jnp.bfloat16),
            pltpu.SemaphoreType.DMA((tiles, blocks)),
        ],
        name="local_pass",
    )(block_cols, block_count, panel, block_vals, weight, cotangent)


def sum_kernel(term, total, paired, half, pieces, chunk, whole, pair_sems, out_sems, in_sems):
    chips = term.shape[1]
    grp, dom = lax.axis_index("grp"), lax.axis_index("dom")
    core = dom % 2
    chip = grp * 8 + dom // 2
    mesh_ids = pl.DeviceIdType.MESH
    partner = {"grp": grp, "dom": dom + 1 - 2 * core}

    def ahead(offset):
        x_hi, y = lax.rem(grp // 4 + offset // 32, 2), lax.rem(grp % 4 + (offset // 8) % 4, 4)
        z, x_lo = lax.rem(dom // 4 + (offset // 2) % 4, 4), lax.rem((dom // 2) % 2 + offset % 2, 2)
        return {"grp": x_hi * 4 + y, "dom": z * 4 + x_lo * 2 + core}

    barrier = pltpu.get_barrier_semaphore()
    pl.semaphore_signal(barrier, inc=1, device_id=partner, device_id_type=mesh_ids)

    @pl.loop(1, chips)
    def _(offset):
        pl.semaphore_signal(barrier, inc=1, device_id=ahead(offset), device_id_type=mesh_ids)

    pl.semaphore_wait(barrier, chips)

    swap = pltpu.make_async_remote_copy(
        src_ref=term.at[1 - core], dst_ref=paired, send_sem=pair_sems.at[0], recv_sem=pair_sems.at[1],
        device_id=partner, device_id_type=mesh_ids,
    )
    swap.start()
    swap.wait()
    half[...] = (term[core].astype(jnp.float32) + paired[...].astype(jnp.float32)).astype(half.dtype)

    def place(offset):
        to = ahead(offset)
        return to["grp"] * 8 + to["dom"] // 2

    @pl.loop(1, chips)
    def _(offset):
        pltpu.make_async_remote_copy(
            src_ref=half.at[place(offset)], dst_ref=pieces.at[offset - 1],
            send_sem=out_sems.at[0], recv_sem=in_sems.at[0],
            device_id=ahead(offset), device_id_type=mesh_ids,
        ).start()

    def all_pieces(number):
        return pltpu.make_async_remote_copy(
            src_ref=pieces, dst_ref=pieces, send_sem=out_sems.at[number], recv_sem=in_sems.at[number],
            device_id=partner, device_id_type=mesh_ids,
        )

    all_pieces(0).wait_recv()
    summed = half[chip].astype(jnp.float32) + jnp.sum(pieces[...].astype(jnp.float32), axis=0)
    chunk[...] = summed.astype(chunk.dtype)
    all_pieces(0).wait_send()

    @pl.loop(1, chips)
    def _(offset):
        pltpu.make_async_remote_copy(
            src_ref=chunk, dst_ref=whole.at[core, chip],
            send_sem=out_sems.at[1], recv_sem=in_sems.at[1],
            device_id=ahead(offset), device_id_type=mesh_ids,
        ).start()

    whole[core, chip] = chunk[...]
    all_pieces(1).wait_recv()
    give = pltpu.make_async_remote_copy(
        src_ref=whole.at[core], dst_ref=whole.at[core], send_sem=pair_sems.at[2], recv_sem=pair_sems.at[3],
        device_id=partner, device_id_type=mesh_ids,
    )
    give.start()
    total[core] = whole[core]
    give.wait()
    total[1 - core] = whole[1 - core]
    all_pieces(1).wait_send()


def sum_terms(term):
    chips = lax.axis_size("grp") * lax.axis_size("dom") // 2
    _, width_in, columns = term.shape
    share = width_in // chips
    shape = (2, chips, share, columns)
    vmem = pl.BlockSpec(memory_space=pltpu.VMEM)
    whole = pl.pallas_call(
        sum_kernel,
        out_shape=jax.ShapeDtypeStruct(shape, term.dtype),
        in_specs=[vmem],
        out_specs=vmem,
        scratch_shapes=[
            pltpu.VMEM(shape[1:], term.dtype),
            pltpu.VMEM(shape[1:], term.dtype),
            pltpu.VMEM((chips - 1, share, columns), term.dtype),
            pltpu.VMEM((share, columns), term.dtype),
            pltpu.VMEM(shape, term.dtype),
            pltpu.SemaphoreType.DMA((4,)),
            pltpu.SemaphoreType.DMA((2,)),
            pltpu.SemaphoreType.DMA((2,)),
        ],
        compiler_params=pltpu.CompilerParams(collective_id=1, has_side_effects=True),
        name="sum_terms",
    )(term.reshape(shape))
    sides = whole.reshape(2, width_in, columns).astype(jnp.float32)
    return jnp.concatenate([sides[0], sides[1]], axis=1)


def shards(features, node_order, block_cols, block_count, block_vals, weight, cotangent):
    ordered = regroup(features, node_order)
    everyone = gather_group(ordered)
    hidden, term = local_pass(everyone, block_cols, block_count, block_vals, weight, cotangent)
    return (hidden, sum_terms(term))


def solution(mesh):
    placed = (
        P(AXES, None),
        P(AXES),
        P(AXES, None),
        P(AXES),
        P(AXES, None, None, None),
        P(),
        P(AXES, None),
    )
    return jax.shard_map(
        shards,
        mesh=mesh,
        in_specs=placed,
        out_specs=(P(AXES, None), P()),
        check_vma=False,
    )
```

```python
import jax
import jax.numpy as jnp
from jax import lax
from jax.experimental import pallas as pl
from jax.experimental.pallas import tpu as pltpu
from jax.sharding import PartitionSpec as P

AXES = ("grp", "dom")


def order_kernel(order, asked, orders, keep_sem, out_sem, in_sem):
    devices, _, rows = orders.shape
    grp, dom = lax.axis_index("grp"), lax.axis_index("dom")
    me = grp * 16 + dom
    mesh_ids = pl.DeviceIdType.MESH

    def ahead(offset):
        x_hi, y = lax.rem(grp // 4 + offset // 64, 2), lax.rem(grp % 4 + (offset // 16) % 4, 4)
        z, x_lo = lax.rem(dom // 4 + (offset // 4) % 4, 4), lax.rem((dom // 2) % 2 + (offset // 2) % 2, 2)
        return {"grp": x_hi * 4 + y, "dom": z * 4 + x_lo * 2 + lax.rem(dom % 2 + offset % 2, 2)}

    barrier = pltpu.get_barrier_semaphore()

    @pl.loop(1, devices)
    def _(offset):
        pl.semaphore_signal(barrier, inc=1, device_id=ahead(offset), device_id_type=mesh_ids)

    keep = pltpu.make_async_copy(order, orders.at[me], keep_sem)
    keep.start()
    pl.semaphore_wait(barrier, devices - 1)

    @pl.loop(1, devices)
    def _(offset):
        pltpu.make_async_remote_copy(
            src_ref=order, dst_ref=orders.at[me], send_sem=out_sem, recv_sem=in_sem,
            device_id=ahead(offset), device_id_type=mesh_ids,
        ).start()

    keep.wait()
    others = orders.at[pl.ds(0, devices - 1)]
    every = pltpu.make_async_remote_copy(
        src_ref=others, dst_ref=others, send_sem=out_sem, recv_sem=in_sem,
        device_id=ahead(1), device_id_type=mesh_ids,
    )
    every.wait_recv()
    row = orders[...].reshape(devices, rows) - me * rows
    mine = jnp.logical_and(row >= 0, row < rows)
    earlier = lax.broadcasted_iota(jnp.int32, (rows, rows), 0) <= lax.broadcasted_iota(jnp.int32, (rows, rows), 1)
    rank = jnp.dot(
        jnp.where(mine, 1.0, 0.0).astype(jnp.bfloat16),
        jnp.where(earlier, 1.0, 0.0).astype(jnp.bfloat16),
        preferred_element_type=jnp.float32,
    )
    rank = jnp.where(mine, rank, 0.0)
    lane = lax.broadcasted_iota(jnp.int32, asked.shape, 1)
    table = jnp.zeros(asked.shape, jnp.float32)
    for number in range(rows // devices):
        picked = jnp.where(rank == number + 1.0, row.astype(jnp.float32), 0.0)
        table = jnp.where(lane == number, jnp.sum(picked, axis=1, keepdims=True), table)
    asked[...] = table.astype(jnp.int32)
    every.wait_send()


def ask(node_order):
    devices = lax.axis_size("grp") * lax.axis_size("dom")
    rows = node_order.shape[0]
    vmem = pl.BlockSpec(memory_space=pltpu.VMEM)
    return pl.pallas_call(
        order_kernel,
        out_shape=jax.ShapeDtypeStruct((devices, 128), jnp.int32),
        in_specs=[vmem],
        out_specs=vmem,
        scratch_shapes=[
            pltpu.VMEM((devices, 1, rows), jnp.int32),
            pltpu.SemaphoreType.DMA,
            pltpu.SemaphoreType.DMA,
            pltpu.SemaphoreType.DMA,
        ],
        compiler_params=pltpu.CompilerParams(collective_id=2, has_side_effects=True),
        name="ask",
    )(node_order.reshape(1, rows))


def regroup(features, node_order):
    row_count, width_in = features.shape
    devices = lax.axis_size("grp") * lax.axis_size("dom")
    per_pair = row_count // devices
    asked_rows = ask(node_order)[:, :per_pair]
    outgoing = features[asked_rows.reshape(-1)].reshape(devices, per_pair, width_in)
    arrived = lax.all_to_all(outgoing, AXES, split_axis=0, concat_axis=0, tiled=True)
    arrived = arrived.reshape(row_count, width_in)
    source = node_order // row_count
    position = jnp.arange(row_count, dtype=jnp.int32)
    before = jnp.logical_and(source[:, None] == source[None, :], position[None, :] < position[:, None])
    slot = source * per_pair + jnp.sum(before.astype(jnp.int32), axis=1)
    return arrived[slot]


def piece_plan(rows):
    half = rows // 2
    cut = rows * 11 // 32
    upper = rows - cut
    up = [
        (0, -1, 0, half, None), (0, -1, half, rows, None), (0, 2, 0, half, ("up", 0)),
        (1, -1, 0, cut, ("side", 0)), (1, 2, cut, half, ("side", 2)), (1, 2, 0, cut, ("up", 3)),
    ]
    down = [
        (0, 1, half, rows, None), (0, 1, 0, half, None), (0, 2, half, rows, ("down", 0)),
        (1, 1, upper, rows, ("side", 1)), (1, 2, half, upper, ("side", 3)), (1, 2, upper, rows, ("down", 3)),
    ]
    side = [
        (1, 0, 0, half, None), (1, 0, half, rows, None), (1, -1, cut, half, ("up", 0)),
        (1, 1, half, upper, ("down", 0)), (1, -1, half, rows, ("up", 1)), (1, 1, 0, half, ("down", 1)),
    ]
    return {"up": up, "down": down, "side": side}


ARRIVALS = (
    ("up", 0), ("down", 0), ("side", 0), ("up", 1), ("down", 1), ("side", 1), ("side", 2), ("side", 3),
    ("up", 2), ("down", 2), ("side", 4), ("up", 3), ("down", 3), ("up", 4), ("down", 4), ("side", 5),
    ("up", 5), ("down", 5),
)
LINKS = ("up", "down", "side")


def gather_kernel(own, out, send_sems, recv_sems, pass_send, pass_recv, keep_sem):
    rows = own.shape[0]
    me = lax.axis_index("dom")
    depth, column, core = me // 4, (me // 2) % 2, me % 2

    def place(other_column, shift, which_core):
        z = lax.rem(depth + shift + 4, 4)
        x = column + other_column * (1 - 2 * column)
        return z * 4 + x * 2 + which_core

    partner = place(0, 0, 1 - core)
    targets = {"up": place(0, 1, core), "down": place(0, -1, core), "side": place(1, 0, core)}

    barrier = pltpu.get_barrier_semaphore()
    for target in (*targets.values(), partner):
        pl.semaphore_signal(barrier, inc=1, device_id={"dom": target}, device_id_type=pl.DeviceIdType.MESH)
    keep = pltpu.make_async_copy(own, out.at[me], keep_sem)
    keep.start()
    pl.semaphore_wait(barrier, 4)

    plan = piece_plan(rows)
    moved = {"up": (0, 1), "down": (0, -1), "side": (1, 0)}

    def send(link, number):
        other, shift, low, high, _ = plan[link][number]
        jump, step = moved[link]
        span = pl.ds(low, high - low)
        source_other, source_shift = (other + jump) % 2, shift + step
        owner = place(source_other, source_shift, core)
        slot = LINKS.index(link) * 6 + number
        block = own.at[span] if plan[link][number][4] is None else out.at[owner, span]
        return pltpu.make_async_remote_copy(
            src_ref=block, dst_ref=out.at[owner, span],
            send_sem=send_sems.at[slot], recv_sem=recv_sems.at[slot],
            device_id={"dom": targets[link]}, device_id_type=pl.DeviceIdType.MESH,
        )

    def landed(link, number):
        other, shift, low, high, _ = plan[link][number]
        span = pl.ds(low, high - low)
        slot = LINKS.index(link) * 6 + number
        here = out.at[place(other, shift, core), span]
        return pltpu.make_async_remote_copy(
            src_ref=here, dst_ref=here,
            send_sem=send_sems.at[slot], recv_sem=recv_sems.at[slot],
            device_id={"dom": targets[link]}, device_id_type=pl.DeviceIdType.MESH,
        )

    def hand_over(number, block, there):
        return pltpu.make_async_remote_copy(
            src_ref=block, dst_ref=there,
            send_sem=pass_send.at[number], recv_sem=pass_recv.at[number],
            device_id={"dom": partner}, device_id_type=pl.DeviceIdType.MESH,
        )

    sent = []
    for number in range(2):
        for link in LINKS:
            copy = send(link, number)
            copy.start()
            sent.append(copy)
    copy = hand_over(18, own, out.at[me])
    copy.start()
    sent.append(copy)

    for order, (link, number) in enumerate(ARRIVALS):
        landed(link, number).wait_recv()
        for onward in LINKS:
            for later in range(2, 6):
                if plan[onward][later][4] == (link, number):
                    copy = send(onward, later)
                    copy.start()
                    sent.append(copy)
        other, shift, low, high, _ = plan[link][number]
        here = out.at[place(other, shift, core), pl.ds(low, high - low)]
        copy = hand_over(order, here, here)
        copy.start()
        sent.append(copy)

    hand_over(18, own, out.at[partner]).wait_recv()
    for order, (link, number) in enumerate(ARRIVALS):
        other, shift, low, high, _ = plan[link][number]
        there = out.at[place(other, shift, 1 - core), pl.ds(low, high - low)]
        hand_over(order, there, there).wait_recv()
    for copy in sent:
        copy.wait_send()
    keep.wait()


def gather_group(ordered):
    rows, width_in = ordered.shape
    group = lax.axis_size("dom")
    return pl.pallas_call(
        gather_kernel,
        out_shape=jax.ShapeDtypeStruct((group, rows, width_in), ordered.dtype),
        in_specs=[pl.BlockSpec(memory_space=pltpu.VMEM)],
        out_specs=pl.BlockSpec(memory_space=pl.ANY),
        scratch_shapes=[
            pltpu.SemaphoreType.DMA((18,)),
            pltpu.SemaphoreType.DMA((18,)),
            pltpu.SemaphoreType.DMA((19,)),
            pltpu.SemaphoreType.DMA((19,)),
            pltpu.SemaphoreType.DMA,
        ],
        compiler_params=pltpu.CompilerParams(collective_id=0, has_side_effects=True),
        name="gather_group",
    )(ordered)


def local_kernel(cols, count, panel, vals, weight, cot, hidden, term, chosen, acc, mixed, sems):
    tiles, blocks, size, _ = vals.shape

    def fetch(t, k):
        return pltpu.make_async_copy(panel.at[cols[t, k]], chosen.at[t, k], sems.at[t, k])

    for t in range(tiles):
        @pl.loop(0, count[t])
        def _(k):
            fetch(t, k).start()

    for t in range(tiles):
        live = count[t]
        fetch(t, 0).wait()
        acc[...] = jnp.dot(vals[t, 0], chosen[t, 0], preferred_element_type=jnp.float32)

        @pl.loop(1, live)
        def _(k):
            fetch(t, k).wait()
            acc[...] += jnp.dot(vals[t, k], chosen[t, k], preferred_element_type=jnp.float32)

        mixed[pl.ds(t * size, size), :] = acc[...].astype(jnp.bfloat16)

    rows = mixed[...]
    aggregate = jnp.dot(rows, weight[...], preferred_element_type=jnp.float32)
    sig = jax.nn.sigmoid(aggregate)
    hidden[...] = (aggregate * sig).astype(hidden.dtype)
    slope = sig * (1.0 + aggregate * (1.0 - sig))
    grad_agg = (cot[...].astype(jnp.float32) * slope).astype(jnp.bfloat16)
    products = lax.dot_general(
        rows, grad_agg, (((0,), (0,)), ((), ())), preferred_element_type=jnp.float32
    ).astype(term.dtype)
    columns = term.shape[2]
    for side in range(2):
        term[side] = products[:, side * columns:(side + 1) * columns]


def local_pass(everyone, block_cols, block_count, block_vals, weight, cotangent):
    tiles, blocks, size, _ = block_vals.shape
    rows, hidden_units = cotangent.shape
    width_in = weight.shape[0]
    panel = everyone.reshape(-1, size, width_in)
    vmem = pl.BlockSpec(memory_space=pltpu.VMEM)
    smem = pl.BlockSpec(memory_space=pltpu.SMEM)
    return pl.pallas_call(
        local_kernel,
        out_shape=(
            jax.ShapeDtypeStruct((rows, hidden_units), jnp.bfloat16),
            jax.ShapeDtypeStruct((2, width_in, hidden_units // 2), jnp.bfloat16),
        ),
        in_specs=[smem, smem, pl.BlockSpec(memory_space=pl.ANY), vmem, vmem, vmem],
        out_specs=(vmem, vmem),
        scratch_shapes=[
            pltpu.VMEM((tiles, blocks, size, width_in), jnp.bfloat16),
            pltpu.VMEM((size, width_in), jnp.float32),
            pltpu.VMEM((rows, width_in), jnp.bfloat16),
            pltpu.SemaphoreType.DMA((tiles, blocks)),
        ],
        name="local_pass",
    )(block_cols, block_count, panel, block_vals, weight, cotangent)


def sum_kernel(term, total, paired, half, pieces, chunk, whole, pair_sems, out_sems, in_sems):
    chips = term.shape[1]
    grp, dom = lax.axis_index("grp"), lax.axis_index("dom")
    core = dom % 2
    chip = grp * 8 + dom // 2
    mesh_ids = pl.DeviceIdType.MESH
    partner = {"grp": grp, "dom": dom + 1 - 2 * core}

    def ahead(offset):
        x_hi, y = lax.rem(grp // 4 + offset // 32, 2), lax.rem(grp % 4 + (offset // 8) % 4, 4)
        z, x_lo = lax.rem(dom // 4 + (offset // 2) % 4, 4), lax.rem((dom // 2) % 2 + offset % 2, 2)
        return {"grp": x_hi * 4 + y, "dom": z * 4 + x_lo * 2 + core}

    barrier = pltpu.get_barrier_semaphore()
    pl.semaphore_signal(barrier, inc=1, device_id=partner, device_id_type=mesh_ids)

    @pl.loop(1, chips)
    def _(offset):
        pl.semaphore_signal(barrier, inc=1, device_id=ahead(offset), device_id_type=mesh_ids)

    pl.semaphore_wait(barrier, chips)

    swap = pltpu.make_async_remote_copy(
        src_ref=term.at[1 - core], dst_ref=paired, send_sem=pair_sems.at[0], recv_sem=pair_sems.at[1],
        device_id=partner, device_id_type=mesh_ids,
    )
    swap.start()
    swap.wait()
    half[...] = (term[core].astype(jnp.float32) + paired[...].astype(jnp.float32)).astype(half.dtype)

    def place(offset):
        to = ahead(offset)
        return to["grp"] * 8 + to["dom"] // 2

    @pl.loop(1, chips)
    def _(offset):
        pltpu.make_async_remote_copy(
            src_ref=half.at[place(offset)], dst_ref=pieces.at[offset - 1],
            send_sem=out_sems.at[0], recv_sem=in_sems.at[0],
            device_id=ahead(offset), device_id_type=mesh_ids,
        ).start()

    def all_pieces(number):
        return pltpu.make_async_remote_copy(
            src_ref=pieces, dst_ref=pieces, send_sem=out_sems.at[number], recv_sem=in_sems.at[number],
            device_id=partner, device_id_type=mesh_ids,
        )

    all_pieces(0).wait_recv()
    summed = half[chip].astype(jnp.float32) + jnp.sum(pieces[...].astype(jnp.float32), axis=0)
    chunk[...] = summed.astype(chunk.dtype)
    all_pieces(0).wait_send()

    @pl.loop(1, chips)
    def _(offset):
        pltpu.make_async_remote_copy(
            src_ref=chunk, dst_ref=whole.at[core, chip],
            send_sem=out_sems.at[1], recv_sem=in_sems.at[1],
            device_id=ahead(offset), device_id_type=mesh_ids,
        ).start()

    whole[core, chip] = chunk[...]
    all_pieces(1).wait_recv()
    give = pltpu.make_async_remote_copy(
        src_ref=whole.at[core], dst_ref=whole.at[core], send_sem=pair_sems.at[2], recv_sem=pair_sems.at[3],
        device_id=partner, device_id_type=mesh_ids,
    )
    give.start()
    give.wait()
    columns = whole.shape[3]
    for side in range(2):
        total[:, :, side * columns:(side + 1) * columns] = whole[side]
    all_pieces(1).wait_send()


def sum_terms(term):
    chips = lax.axis_size("grp") * lax.axis_size("dom") // 2
    _, width_in, columns = term.shape
    share = width_in // chips
    shape = (2, chips, share, columns)
    vmem = pl.BlockSpec(memory_space=pltpu.VMEM)
    whole = pl.pallas_call(
        sum_kernel,
        out_shape=jax.ShapeDtypeStruct((chips, share, 2 * columns), term.dtype),
        in_specs=[vmem],
        out_specs=vmem,
        scratch_shapes=[
            pltpu.VMEM(shape[1:], term.dtype),
            pltpu.VMEM(shape[1:], term.dtype),
            pltpu.VMEM((chips - 1, share, columns), term.dtype),
            pltpu.VMEM((share, columns), term.dtype),
            pltpu.VMEM(shape, term.dtype),
            pltpu.SemaphoreType.DMA((4,)),
            pltpu.SemaphoreType.DMA((2,)),
            pltpu.SemaphoreType.DMA((2,)),
        ],
        compiler_params=pltpu.CompilerParams(collective_id=1, has_side_effects=True),
        name="sum_terms",
    )(term.reshape(shape))
    return whole.reshape(width_in, 2 * columns).astype(jnp.float32)


def shards(features, node_order, block_cols, block_count, block_vals, weight, cotangent):
    ordered = regroup(features, node_order)
    everyone = gather_group(ordered)
    hidden, term = local_pass(everyone, block_cols, block_count, block_vals, weight, cotangent)
    return (hidden, sum_terms(term))


def solution(mesh):
    placed = (
        P(AXES, None),
        P(AXES),
        P(AXES, None),
        P(AXES),
        P(AXES, None, None, None),
        P(),
        P(AXES, None),
    )
    return jax.shard_map(
        shards,
        mesh=mesh,
        in_specs=placed,
        out_specs=(P(AXES, None), P()),
        check_vma=False,
    )
```

```python
import jax
import jax.numpy as jnp
from jax import lax
from jax.experimental import pallas as pl
from jax.experimental.pallas import tpu as pltpu
from jax.sharding import PartitionSpec as P

AXES = ("grp", "dom")


def order_kernel(order, asked, orders, keep_sem, out_sems, in_sems):
    group, groups, _, rows = orders.shape
    grp, dom = lax.axis_index("grp"), lax.axis_index("dom")
    mesh_ids = pl.DeviceIdType.MESH

    def across(offset):
        x_hi, y = lax.rem(grp // 4 + offset // 4, 2), lax.rem(grp % 4 + offset % 4, 4)
        return {"grp": x_hi * 4 + y, "dom": dom}

    def along(offset):
        z, x_lo = lax.rem(dom // 4 + offset // 4, 4), lax.rem((dom // 2) % 2 + (offset // 2) % 2, 2)
        return {"grp": grp, "dom": z * 4 + x_lo * 2 + lax.rem(dom % 2 + offset % 2, 2)}

    barrier = pltpu.get_barrier_semaphore()
    for offset in range(1, groups):
        pl.semaphore_signal(barrier, inc=1, device_id=across(offset), device_id_type=mesh_ids)
    for offset in range(1, group):
        pl.semaphore_signal(barrier, inc=1, device_id=along(offset), device_id_type=mesh_ids)
    keep = pltpu.make_async_copy(order, orders.at[dom, grp], keep_sem)
    keep.start()
    pl.semaphore_wait(barrier, groups + group - 2)

    for offset in range(1, groups):
        pltpu.make_async_remote_copy(
            src_ref=order, dst_ref=orders.at[dom, grp], send_sem=out_sems.at[0], recv_sem=in_sems.at[0],
            device_id=across(offset), device_id_type=mesh_ids,
        ).start()
    keep.wait()
    some = orders.at[0, pl.ds(0, groups - 1)]
    first = pltpu.make_async_remote_copy(
        src_ref=some, dst_ref=some, send_sem=out_sems.at[0], recv_sem=in_sems.at[0],
        device_id=across(1), device_id_type=mesh_ids,
    )
    first.wait_recv()
    for offset in range(1, group):
        pltpu.make_async_remote_copy(
            src_ref=orders.at[dom], dst_ref=orders.at[dom], send_sem=out_sems.at[1], recv_sem=in_sems.at[1],
            device_id=along(offset), device_id_type=mesh_ids,
        ).start()
    others = orders.at[pl.ds(0, group - 1)]
    every = pltpu.make_async_remote_copy(
        src_ref=others, dst_ref=others, send_sem=out_sems.at[1], recv_sem=in_sems.at[1],
        device_id=along(1), device_id_type=mesh_ids,
    )
    every.wait_recv()
    row = jnp.concatenate([orders[:, number].reshape(group, rows) for number in range(groups)], axis=0)
    row = row - (grp * group + dom) * rows
    mine = jnp.logical_and(row >= 0, row < rows)
    earlier = lax.broadcasted_iota(jnp.int32, (rows, rows), 0) <= lax.broadcasted_iota(jnp.int32, (rows, rows), 1)
    rank = jnp.dot(
        jnp.where(mine, 1.0, 0.0).astype(jnp.bfloat16),
        jnp.where(earlier, 1.0, 0.0).astype(jnp.bfloat16),
        preferred_element_type=jnp.float32,
    )
    rank = jnp.where(mine, rank, 0.0)
    lane = lax.broadcasted_iota(jnp.int32, asked.shape, 1)
    table = jnp.zeros(asked.shape, jnp.float32)
    for number in range(rows // (groups * group)):
        picked = jnp.where(rank == number + 1.0, row.astype(jnp.float32), 0.0)
        table = jnp.where(lane == number, jnp.sum(picked, axis=1, keepdims=True), table)
    asked[...] = table.astype(jnp.int32)
    first.wait_send()
    every.wait_send()


def ask(node_order):
    devices = lax.axis_size("grp") * lax.axis_size("dom")
    rows = node_order.shape[0]
    vmem = pl.BlockSpec(memory_space=pltpu.VMEM)
    return pl.pallas_call(
        order_kernel,
        out_shape=jax.ShapeDtypeStruct((devices, 128), jnp.int32),
        in_specs=[vmem],
        out_specs=vmem,
        scratch_shapes=[
            pltpu.VMEM((lax.axis_size("dom"), lax.axis_size("grp"), 1, rows), jnp.int32),
            pltpu.SemaphoreType.DMA,
            pltpu.SemaphoreType.DMA((2,)),
            pltpu.SemaphoreType.DMA((2,)),
        ],
        compiler_params=pltpu.CompilerParams(collective_id=2, has_side_effects=True),
        name="ask",
    )(node_order.reshape(1, rows))


def regroup(features, node_order):
    row_count, width_in = features.shape
    devices = lax.axis_size("grp") * lax.axis_size("dom")
    per_pair = row_count // devices
    asked_rows = ask(node_order)[:, :per_pair]
    outgoing = features[asked_rows.reshape(-1)].reshape(devices, per_pair, width_in)
    arrived = lax.all_to_all(outgoing, AXES, split_axis=0, concat_axis=0, tiled=True)
    arrived = arrived.reshape(row_count, width_in)
    source = node_order // row_count
    position = jnp.arange(row_count, dtype=jnp.int32)
    before = jnp.logical_and(source[:, None] == source[None, :], position[None, :] < position[:, None])
    slot = source * per_pair + jnp.sum(before.astype(jnp.int32), axis=1)
    return arrived, slot


def piece_plan(rows):
    half = rows // 2
    cut = rows * 11 // 32
    upper = rows - cut
    up = [
        (0, -1, 0, half, None), (0, -1, half, rows, None), (0, 2, 0, half, ("up", 0)),
        (1, -1, 0, cut, ("side", 0)), (1, 2, cut, half, ("side", 2)), (1, 2, 0, cut, ("up", 3)),
    ]
    down = [
        (0, 1, half, rows, None), (0, 1, 0, half, None), (0, 2, half, rows, ("down", 0)),
        (1, 1, upper, rows, ("side", 1)), (1, 2, half, upper, ("side", 3)), (1, 2, upper, rows, ("down", 3)),
    ]
    side = [
        (1, 0, 0, half, None), (1, 0, half, rows, None), (1, -1, cut, half, ("up", 0)),
        (1, 1, half, upper, ("down", 0)), (1, -1, half, rows, ("up", 1)), (1, 1, 0, half, ("down", 1)),
    ]
    return {"up": up, "down": down, "side": side}


ARRIVALS = (
    ("up", 0), ("down", 0), ("side", 0), ("up", 1), ("down", 1), ("side", 1), ("side", 2), ("side", 3),
    ("up", 2), ("down", 2), ("side", 4), ("up", 3), ("down", 3), ("up", 4), ("down", 4), ("side", 5),
    ("up", 5), ("down", 5),
)
LINKS = ("up", "down", "side")


def gather_kernel(arrived, slot, out, own, send_sems, recv_sems, pass_send, pass_recv, keep_sem):
    rows = own.shape[0]
    me = lax.axis_index("dom")
    depth, column, core = me // 4, (me // 2) % 2, me % 2

    def place(other_column, shift, which_core):
        z = lax.rem(depth + shift + 4, 4)
        x = column + other_column * (1 - 2 * column)
        return z * 4 + x * 2 + which_core

    partner = place(0, 0, 1 - core)
    targets = {"up": place(0, 1, core), "down": place(0, -1, core), "side": place(1, 0, core)}

    barrier = pltpu.get_barrier_semaphore()
    for target in (*targets.values(), partner):
        pl.semaphore_signal(barrier, inc=1, device_id={"dom": target}, device_id_type=pl.DeviceIdType.MESH)
    taken = lax.broadcasted_iota(jnp.int32, (rows, rows), 0) == slot[...]
    own[...] = lax.dot_general(
        jnp.where(taken, 1.0, 0.0).astype(own.dtype), arrived[...],
        (((0,), (0,)), ((), ())), preferred_element_type=jnp.float32,
    ).astype(own.dtype)
    keep = pltpu.make_async_copy(own, out.at[me], keep_sem)
    keep.start()
    pl.semaphore_wait(barrier, 4)

    plan = piece_plan(rows)
    moved = {"up": (0, 1), "down": (0, -1), "side": (1, 0)}

    def send(link, number):
        other, shift, low, high, _ = plan[link][number]
        jump, step = moved[link]
        span = pl.ds(low, high - low)
        source_other, source_shift = (other + jump) % 2, shift + step
        owner = place(source_other, source_shift, core)
        slot = LINKS.index(link) * 6 + number
        block = own.at[span] if plan[link][number][4] is None else out.at[owner, span]
        return pltpu.make_async_remote_copy(
            src_ref=block, dst_ref=out.at[owner, span],
            send_sem=send_sems.at[slot], recv_sem=recv_sems.at[slot],
            device_id={"dom": targets[link]}, device_id_type=pl.DeviceIdType.MESH,
        )

    def landed(link, number):
        other, shift, low, high, _ = plan[link][number]
        span = pl.ds(low, high - low)
        slot = LINKS.index(link) * 6 + number
        here = out.at[place(other, shift, core), span]
        return pltpu.make_async_remote_copy(
            src_ref=here, dst_ref=here,
            send_sem=send_sems.at[slot], recv_sem=recv_sems.at[slot],
            device_id={"dom": targets[link]}, device_id_type=pl.DeviceIdType.MESH,
        )

    def hand_over(number, block, there):
        return pltpu.make_async_remote_copy(
            src_ref=block, dst_ref=there,
            send_sem=pass_send.at[number], recv_sem=pass_recv.at[number],
            device_id={"dom": partner}, device_id_type=pl.DeviceIdType.MESH,
        )

    sent = []
    for number in range(2):
        for link in LINKS:
            copy = send(link, number)
            copy.start()
            sent.append(copy)
    copy = hand_over(18, own, out.at[me])
    copy.start()
    sent.append(copy)

    for order, (link, number) in enumerate(ARRIVALS):
        landed(link, number).wait_recv()
        for onward in LINKS:
            for later in range(2, 6):
                if plan[onward][later][4] == (link, number):
                    copy = send(onward, later)
                    copy.start()
                    sent.append(copy)
        other, shift, low, high, _ = plan[link][number]
        here = out.at[place(other, shift, core), pl.ds(low, high - low)]
        copy = hand_over(order, here, here)
        copy.start()
        sent.append(copy)

    hand_over(18, own, out.at[partner]).wait_recv()
    for order, (link, number) in enumerate(ARRIVALS):
        other, shift, low, high, _ = plan[link][number]
        there = out.at[place(other, shift, 1 - core), pl.ds(low, high - low)]
        hand_over(order, there, there).wait_recv()
    for copy in sent:
        copy.wait_send()
    keep.wait()


def gather_group(arrived, slot):
    rows, width_in = arrived.shape
    vmem = pl.BlockSpec(memory_space=pltpu.VMEM)
    group = lax.axis_size("dom")
    return pl.pallas_call(
        gather_kernel,
        out_shape=jax.ShapeDtypeStruct((group, rows, width_in), arrived.dtype),
        in_specs=[vmem, vmem],
        out_specs=pl.BlockSpec(memory_space=pl.ANY),
        scratch_shapes=[
            pltpu.VMEM((rows, width_in), arrived.dtype),
            pltpu.SemaphoreType.DMA((18,)),
            pltpu.SemaphoreType.DMA((18,)),
            pltpu.SemaphoreType.DMA((19,)),
            pltpu.SemaphoreType.DMA((19,)),
            pltpu.SemaphoreType.DMA,
        ],
        compiler_params=pltpu.CompilerParams(collective_id=0, has_side_effects=True),
        name="gather_group",
    )(arrived, slot.reshape(1, rows))


def local_kernel(cols, count, panel, vals, weight, cot, hidden, term, chosen, acc, mixed, sems):
    tiles, blocks, size, _ = vals.shape

    def fetch(t, k):
        return pltpu.make_async_copy(panel.at[cols[t, k]], chosen.at[t, k], sems.at[t, k])

    for t in range(tiles):
        @pl.loop(0, count[t])
        def _(k):
            fetch(t, k).start()

    for t in range(tiles):
        live = count[t]
        fetch(t, 0).wait()
        acc[...] = jnp.dot(vals[t, 0], chosen[t, 0], preferred_element_type=jnp.float32)

        @pl.loop(1, live)
        def _(k):
            fetch(t, k).wait()
            acc[...] += jnp.dot(vals[t, k], chosen[t, k], preferred_element_type=jnp.float32)

        mixed[pl.ds(t * size, size), :] = acc[...].astype(jnp.bfloat16)

    rows = mixed[...]
    aggregate = jnp.dot(rows, weight[...], preferred_element_type=jnp.float32)
    sig = jax.nn.sigmoid(aggregate)
    hidden[...] = (aggregate * sig).astype(hidden.dtype)
    slope = sig * (1.0 + aggregate * (1.0 - sig))
    grad_agg = (cot[...].astype(jnp.float32) * slope).astype(jnp.bfloat16)
    products = lax.dot_general(
        rows, grad_agg, (((0,), (0,)), ((), ())), preferred_element_type=jnp.float32
    ).astype(term.dtype)
    columns = term.shape[2]
    for side in range(2):
        term[side] = products[:, side * columns:(side + 1) * columns]


def local_pass(everyone, block_cols, block_count, block_vals, weight, cotangent):
    tiles, blocks, size, _ = block_vals.shape
    rows, hidden_units = cotangent.shape
    width_in = weight.shape[0]
    panel = everyone.reshape(-1, size, width_in)
    vmem = pl.BlockSpec(memory_space=pltpu.VMEM)
    smem = pl.BlockSpec(memory_space=pltpu.SMEM)
    return pl.pallas_call(
        local_kernel,
        out_shape=(
            jax.ShapeDtypeStruct((rows, hidden_units), jnp.bfloat16),
            jax.ShapeDtypeStruct((2, width_in, hidden_units // 2), jnp.bfloat16),
        ),
        in_specs=[smem, smem, pl.BlockSpec(memory_space=pl.ANY), vmem, vmem, vmem],
        out_specs=(vmem, vmem),
        scratch_shapes=[
            pltpu.VMEM((tiles, blocks, size, width_in), jnp.bfloat16),
            pltpu.VMEM((size, width_in), jnp.float32),
            pltpu.VMEM((rows, width_in), jnp.bfloat16),
            pltpu.SemaphoreType.DMA((tiles, blocks)),
        ],
        name="local_pass",
    )(block_cols, block_count, panel, block_vals, weight, cotangent)


def sum_kernel(term, total, paired, half, pieces, chunk, whole, pair_sems, out_sems, in_sems):
    chips = term.shape[1]
    grp, dom = lax.axis_index("grp"), lax.axis_index("dom")
    core = dom % 2
    chip = grp * 8 + dom // 2
    mesh_ids = pl.DeviceIdType.MESH
    partner = {"grp": grp, "dom": dom + 1 - 2 * core}

    def ahead(offset):
        x_hi, y = lax.rem(grp // 4 + offset // 32, 2), lax.rem(grp % 4 + (offset // 8) % 4, 4)
        z, x_lo = lax.rem(dom // 4 + (offset // 2) % 4, 4), lax.rem((dom // 2) % 2 + offset % 2, 2)
        return {"grp": x_hi * 4 + y, "dom": z * 4 + x_lo * 2 + core}

    barrier = pltpu.get_barrier_semaphore()
    pl.semaphore_signal(barrier, inc=1, device_id=partner, device_id_type=mesh_ids)

    @pl.loop(1, chips)
    def _(offset):
        pl.semaphore_signal(barrier, inc=1, device_id=ahead(offset), device_id_type=mesh_ids)

    pl.semaphore_wait(barrier, chips)

    swap = pltpu.make_async_remote_copy(
        src_ref=term.at[1 - core], dst_ref=paired, send_sem=pair_sems.at[0], recv_sem=pair_sems.at[1],
        device_id=partner, device_id_type=mesh_ids,
    )
    swap.start()
    swap.wait()
    half[...] = (term[core].astype(jnp.float32) + paired[...].astype(jnp.float32)).astype(half.dtype)

    def place(offset):
        to = ahead(offset)
        return to["grp"] * 8 + to["dom"] // 2

    @pl.loop(1, chips)
    def _(offset):
        pltpu.make_async_remote_copy(
            src_ref=half.at[place(offset)], dst_ref=pieces.at[offset - 1],
            send_sem=out_sems.at[0], recv_sem=in_sems.at[0],
            device_id=ahead(offset), device_id_type=mesh_ids,
        ).start()

    def all_pieces(number):
        return pltpu.make_async_remote_copy(
            src_ref=pieces, dst_ref=pieces, send_sem=out_sems.at[number], recv_sem=in_sems.at[number],
            device_id=partner, device_id_type=mesh_ids,
        )

    all_pieces(0).wait_recv()
    summed = half[chip].astype(jnp.float32) + jnp.sum(pieces[...].astype(jnp.float32), axis=0)
    chunk[...] = summed.astype(chunk.dtype)
    all_pieces(0).wait_send()

    @pl.loop(1, chips)
    def _(offset):
        pltpu.make_async_remote_copy(
            src_ref=chunk, dst_ref=whole.at[core, chip],
            send_sem=out_sems.at[1], recv_sem=in_sems.at[1],
            device_id=ahead(offset), device_id_type=mesh_ids,
        ).start()

    whole[core, chip] = chunk[...]
    all_pieces(1).wait_recv()
    give = pltpu.make_async_remote_copy(
        src_ref=whole.at[core], dst_ref=whole.at[core], send_sem=pair_sems.at[2], recv_sem=pair_sems.at[3],
        device_id=partner, device_id_type=mesh_ids,
    )
    give.start()
    give.wait()
    columns = whole.shape[3]
    for side in range(2):
        total[:, :, side * columns:(side + 1) * columns] = whole[side]
    all_pieces(1).wait_send()


def sum_terms(term):
    chips = lax.axis_size("grp") * lax.axis_size("dom") // 2
    _, width_in, columns = term.shape
    share = width_in // chips
    shape = (2, chips, share, columns)
    vmem = pl.BlockSpec(memory_space=pltpu.VMEM)
    whole = pl.pallas_call(
        sum_kernel,
        out_shape=jax.ShapeDtypeStruct((chips, share, 2 * columns), term.dtype),
        in_specs=[vmem],
        out_specs=vmem,
        scratch_shapes=[
            pltpu.VMEM(shape[1:], term.dtype),
            pltpu.VMEM(shape[1:], term.dtype),
            pltpu.VMEM((chips - 1, share, columns), term.dtype),
            pltpu.VMEM((share, columns), term.dtype),
            pltpu.VMEM(shape, term.dtype),
            pltpu.SemaphoreType.DMA((4,)),
            pltpu.SemaphoreType.DMA((2,)),
            pltpu.SemaphoreType.DMA((2,)),
        ],
        compiler_params=pltpu.CompilerParams(collective_id=1, has_side_effects=True),
        name="sum_terms",
    )(term.reshape(shape))
    return whole.reshape(width_in, 2 * columns).astype(jnp.float32)


def shards(features, node_order, block_cols, block_count, block_vals, weight, cotangent):
    arrived, slot = regroup(features, node_order)
    everyone = gather_group(arrived, slot)
    hidden, term = local_pass(everyone, block_cols, block_count, block_vals, weight, cotangent)
    return (hidden, sum_terms(term))


def solution(mesh):
    placed = (
        P(AXES, None),
        P(AXES),
        P(AXES, None),
        P(AXES),
        P(AXES, None, None, None),
        P(),
        P(AXES, None),
    )
    return jax.shard_map(
        shards,
        mesh=mesh,
        in_specs=placed,
        out_specs=(P(AXES, None), P()),
        check_vma=False,
    )
```

```python
import jax
import jax.numpy as jnp
from jax import lax
from jax.experimental import pallas as pl
from jax.experimental.pallas import tpu as pltpu
from jax.sharding import PartitionSpec as P

AXES = ("grp", "dom")


def order_kernel(order, asked, orders, keep_sem, out_sems, in_sems):
    group, groups, _, rows = orders.shape
    grp, dom = lax.axis_index("grp"), lax.axis_index("dom")
    mesh_ids = pl.DeviceIdType.MESH

    def across(offset):
        x_hi, y = lax.rem(grp // 4 + offset // 4, 2), lax.rem(grp % 4 + offset % 4, 4)
        return {"grp": x_hi * 4 + y, "dom": dom}

    def along(offset):
        z, x_lo = lax.rem(dom // 4 + offset // 4, 4), lax.rem((dom // 2) % 2 + (offset // 2) % 2, 2)
        return {"grp": grp, "dom": z * 4 + x_lo * 2 + lax.rem(dom % 2 + offset % 2, 2)}

    barrier = pltpu.get_barrier_semaphore()
    for offset in range(1, groups):
        pl.semaphore_signal(barrier, inc=1, device_id=across(offset), device_id_type=mesh_ids)
    for offset in range(1, group):
        pl.semaphore_signal(barrier, inc=1, device_id=along(offset), device_id_type=mesh_ids)
    keep = pltpu.make_async_copy(order, orders.at[dom, grp], keep_sem)
    keep.start()
    pl.semaphore_wait(barrier, groups + group - 2)

    for offset in range(1, groups):
        pltpu.make_async_remote_copy(
            src_ref=order, dst_ref=orders.at[dom, grp], send_sem=out_sems.at[0], recv_sem=in_sems.at[0],
            device_id=across(offset), device_id_type=mesh_ids,
        ).start()
    keep.wait()
    some = orders.at[0, pl.ds(0, groups - 1)]
    first = pltpu.make_async_remote_copy(
        src_ref=some, dst_ref=some, send_sem=out_sems.at[0], recv_sem=in_sems.at[0],
        device_id=across(1), device_id_type=mesh_ids,
    )
    first.wait_recv()
    for offset in range(1, group):
        pltpu.make_async_remote_copy(
            src_ref=orders.at[dom], dst_ref=orders.at[dom], send_sem=out_sems.at[1], recv_sem=in_sems.at[1],
            device_id=along(offset), device_id_type=mesh_ids,
        ).start()
    others = orders.at[pl.ds(0, group - 1)]
    every = pltpu.make_async_remote_copy(
        src_ref=others, dst_ref=others, send_sem=out_sems.at[1], recv_sem=in_sems.at[1],
        device_id=along(1), device_id_type=mesh_ids,
    )
    every.wait_recv()
    row = jnp.concatenate([orders[:, number].reshape(group, rows) for number in range(groups)], axis=0)
    row = row - (grp * group + dom) * rows
    mine = jnp.logical_and(row >= 0, row < rows)
    earlier = lax.broadcasted_iota(jnp.int32, (rows, rows), 0) <= lax.broadcasted_iota(jnp.int32, (rows, rows), 1)
    rank = jnp.dot(
        jnp.where(mine, 1.0, 0.0).astype(jnp.bfloat16),
        jnp.where(earlier, 1.0, 0.0).astype(jnp.bfloat16),
        preferred_element_type=jnp.float32,
    )
    rank = jnp.where(mine, rank, 0.0)
    lane = lax.broadcasted_iota(jnp.int32, asked.shape, 1)
    table = jnp.zeros(asked.shape, jnp.float32)
    for number in range(rows // (groups * group)):
        picked = jnp.where(rank == number + 1.0, row.astype(jnp.float32), 0.0)
        table = jnp.where(lane == number, jnp.sum(picked, axis=1, keepdims=True), table)
    asked[...] = table.astype(jnp.int32)
    first.wait_send()
    every.wait_send()


def ask(node_order):
    devices = lax.axis_size("grp") * lax.axis_size("dom")
    rows = node_order.shape[0]
    vmem = pl.BlockSpec(memory_space=pltpu.VMEM)
    return pl.pallas_call(
        order_kernel,
        out_shape=jax.ShapeDtypeStruct((devices, 128), jnp.int32),
        in_specs=[vmem],
        out_specs=vmem,
        scratch_shapes=[
            pltpu.VMEM((lax.axis_size("dom"), lax.axis_size("grp"), 1, rows), jnp.int32),
            pltpu.SemaphoreType.DMA,
            pltpu.SemaphoreType.DMA((2,)),
            pltpu.SemaphoreType.DMA((2,)),
        ],
        compiler_params=pltpu.CompilerParams(collective_id=2, has_side_effects=True),
        name="ask",
    )(node_order.reshape(1, rows))


def regroup(features, node_order):
    row_count, width_in = features.shape
    devices = lax.axis_size("grp") * lax.axis_size("dom")
    per_pair = row_count // devices
    asked_rows = ask(node_order)[:, :per_pair]
    outgoing = features[asked_rows.reshape(-1)].reshape(devices, per_pair, width_in)
    arrived = lax.all_to_all(outgoing, AXES, split_axis=0, concat_axis=0, tiled=True)
    arrived = arrived.reshape(row_count, width_in)
    source = node_order // row_count
    position = jnp.arange(row_count, dtype=jnp.int32)
    before = jnp.logical_and(source[:, None] == source[None, :], position[None, :] < position[:, None])
    slot = source * per_pair + jnp.sum(before.astype(jnp.int32), axis=1)
    return arrived, slot


def piece_plan(rows):
    half = rows // 2
    cut = rows * 11 // 32
    upper = rows - cut
    up = [
        (0, -1, 0, half, None), (0, -1, half, rows, None), (0, 2, 0, half, ("up", 0)),
        (1, -1, 0, cut, ("side", 0)), (1, 2, cut, half, ("side", 2)), (1, 2, 0, cut, ("up", 3)),
    ]
    down = [
        (0, 1, half, rows, None), (0, 1, 0, half, None), (0, 2, half, rows, ("down", 0)),
        (1, 1, upper, rows, ("side", 1)), (1, 2, half, upper, ("side", 3)), (1, 2, upper, rows, ("down", 3)),
    ]
    side = [
        (1, 0, 0, half, None), (1, 0, half, rows, None), (1, -1, cut, half, ("up", 0)),
        (1, 1, half, upper, ("down", 0)), (1, -1, half, rows, ("up", 1)), (1, 1, 0, half, ("down", 1)),
    ]
    return {"up": up, "down": down, "side": side}


ARRIVALS = (
    ("up", 0), ("down", 0), ("side", 0), ("up", 1), ("down", 1), ("side", 1), ("side", 2), ("side", 3),
    ("up", 2), ("down", 2), ("side", 4), ("up", 3), ("down", 3), ("up", 4), ("down", 4), ("side", 5),
    ("up", 5), ("down", 5),
)
LINKS = ("up", "down", "side")


def gather_kernel(arrived, slot, out, own, send_sems, recv_sems, pass_send, pass_recv, keep_sem):
    rows = own.shape[0]
    me = lax.axis_index("dom")
    depth, column, core = me // 4, (me // 2) % 2, me % 2

    def place(other_column, shift, which_core):
        z = lax.rem(depth + shift + 4, 4)
        x = column + other_column * (1 - 2 * column)
        return z * 4 + x * 2 + which_core

    partner = place(0, 0, 1 - core)
    targets = {"up": place(0, 1, core), "down": place(0, -1, core), "side": place(1, 0, core)}

    barrier = pltpu.get_barrier_semaphore()
    for target in (*targets.values(), partner):
        pl.semaphore_signal(barrier, inc=1, device_id={"dom": target}, device_id_type=pl.DeviceIdType.MESH)
    taken = lax.broadcasted_iota(jnp.int32, (rows, rows), 0) == slot[...]
    own[...] = lax.dot_general(
        jnp.where(taken, 1.0, 0.0).astype(own.dtype), arrived[...],
        (((0,), (0,)), ((), ())), preferred_element_type=jnp.float32,
    ).astype(own.dtype)
    keep = pltpu.make_async_copy(own, out.at[me], keep_sem)
    keep.start()
    pl.semaphore_wait(barrier, 4)

    plan = piece_plan(rows)
    moved = {"up": (0, 1), "down": (0, -1), "side": (1, 0)}

    def send(link, number):
        other, shift, low, high, _ = plan[link][number]
        jump, step = moved[link]
        span = pl.ds(low, high - low)
        source_other, source_shift = (other + jump) % 2, shift + step
        owner = place(source_other, source_shift, core)
        slot = LINKS.index(link) * 6 + number
        block = own.at[span] if plan[link][number][4] is None else out.at[owner, span]
        return pltpu.make_async_remote_copy(
            src_ref=block, dst_ref=out.at[owner, span],
            send_sem=send_sems.at[slot], recv_sem=recv_sems.at[slot],
            device_id={"dom": targets[link]}, device_id_type=pl.DeviceIdType.MESH,
        )

    def landed(link, number):
        other, shift, low, high, _ = plan[link][number]
        span = pl.ds(low, high - low)
        slot = LINKS.index(link) * 6 + number
        here = out.at[place(other, shift, core), span]
        return pltpu.make_async_remote_copy(
            src_ref=here, dst_ref=here,
            send_sem=send_sems.at[slot], recv_sem=recv_sems.at[slot],
            device_id={"dom": targets[link]}, device_id_type=pl.DeviceIdType.MESH,
        )

    def hand_over(number, block, there):
        return pltpu.make_async_remote_copy(
            src_ref=block, dst_ref=there,
            send_sem=pass_send.at[number], recv_sem=pass_recv.at[number],
            device_id={"dom": partner}, device_id_type=pl.DeviceIdType.MESH,
        )

    sent = []
    for number in range(2):
        for link in LINKS:
            copy = send(link, number)
            copy.start()
            sent.append(copy)
    copy = hand_over(18, own, out.at[me])
    copy.start()
    sent.append(copy)

    for order, (link, number) in enumerate(ARRIVALS):
        landed(link, number).wait_recv()
        for onward in LINKS:
            for later in range(2, 6):
                if plan[onward][later][4] == (link, number):
                    copy = send(onward, later)
                    copy.start()
                    sent.append(copy)
        other, shift, low, high, _ = plan[link][number]
        here = out.at[place(other, shift, core), pl.ds(low, high - low)]
        copy = hand_over(order, here, here)
        copy.start()
        sent.append(copy)

    hand_over(18, own, out.at[partner]).wait_recv()
    for order, (link, number) in enumerate(ARRIVALS):
        other, shift, low, high, _ = plan[link][number]
        there = out.at[place(other, shift, 1 - core), pl.ds(low, high - low)]
        hand_over(order, there, there).wait_recv()
    for copy in sent:
        copy.wait_send()
    keep.wait()


def gather_group(arrived, slot):
    rows, width_in = arrived.shape
    vmem = pl.BlockSpec(memory_space=pltpu.VMEM)
    group = lax.axis_size("dom")
    return pl.pallas_call(
        gather_kernel,
        out_shape=jax.ShapeDtypeStruct((group, rows, width_in), arrived.dtype),
        in_specs=[vmem, vmem],
        out_specs=pl.BlockSpec(memory_space=pl.ANY),
        scratch_shapes=[
            pltpu.VMEM((rows, width_in), arrived.dtype),
            pltpu.SemaphoreType.DMA((18,)),
            pltpu.SemaphoreType.DMA((18,)),
            pltpu.SemaphoreType.DMA((19,)),
            pltpu.SemaphoreType.DMA((19,)),
            pltpu.SemaphoreType.DMA,
        ],
        compiler_params=pltpu.CompilerParams(collective_id=0, has_side_effects=True),
        name="gather_group",
    )(arrived, slot.reshape(1, rows))


def local_kernel(cols, count, panel, vals, weight, cot, hidden, mixed, grad, chosen, acc, sems):
    tiles, blocks, size, _ = vals.shape

    def fetch(t, k):
        return pltpu.make_async_copy(panel.at[cols[t, k]], chosen.at[t, k], sems.at[t, k])

    def pairs(t):
        return (count[t] + 1) // 2

    def product(t, pair):
        k = 2 * pair
        fetch(t, k).wait()
        fetch(t, k + 1).wait()
        second = vals[t, k + 1]
        second = jnp.where(k + 1 < count[t], second, jnp.zeros_like(second))
        left = jnp.concatenate([vals[t, k], second], axis=1)
        right = chosen[t, pl.ds(k, 2)].reshape(2 * size, chosen.shape[3])
        return jnp.dot(left, right, preferred_element_type=jnp.float32)

    for t in range(tiles):
        @pl.loop(0, 2 * pairs(t))
        def _(k):
            fetch(t, k).start()

    for t in range(tiles):
        acc[...] = product(t, 0)

        @pl.loop(1, pairs(t))
        def _(pair):
            acc[...] += product(t, pair)

        mixed[pl.ds(t * size, size), :] = acc[...].astype(jnp.bfloat16)

    aggregate = jnp.dot(mixed[...], weight[...], preferred_element_type=jnp.float32)
    sig = jax.nn.sigmoid(aggregate)
    hidden[...] = (aggregate * sig).astype(hidden.dtype)
    slope = sig * (1.0 + aggregate * (1.0 - sig))
    grad_agg = (cot[...].astype(jnp.float32) * slope).astype(grad.dtype)
    columns = grad.shape[2]
    for side in range(2):
        grad[side] = grad_agg[:, side * columns:(side + 1) * columns]


def local_pass(everyone, block_cols, block_count, block_vals, weight, cotangent):
    tiles, blocks, size, _ = block_vals.shape
    rows, hidden_units = cotangent.shape
    width_in = weight.shape[0]
    panel = everyone.reshape(-1, size, width_in)
    vmem = pl.BlockSpec(memory_space=pltpu.VMEM)
    smem = pl.BlockSpec(memory_space=pltpu.SMEM)
    return pl.pallas_call(
        local_kernel,
        out_shape=(
            jax.ShapeDtypeStruct((rows, hidden_units), jnp.bfloat16),
            jax.ShapeDtypeStruct((rows, width_in), jnp.bfloat16),
            jax.ShapeDtypeStruct((2, rows, hidden_units // 2), jnp.bfloat16),
        ),
        in_specs=[smem, smem, pl.BlockSpec(memory_space=pl.ANY), vmem, vmem, vmem],
        out_specs=(vmem, vmem, vmem),
        scratch_shapes=[
            pltpu.VMEM((tiles, blocks, size, width_in), jnp.bfloat16),
            pltpu.VMEM((size, width_in), jnp.float32),
            pltpu.SemaphoreType.DMA((tiles, blocks)),
        ],
        name="local_pass",
    )(block_cols, block_count, panel, block_vals, weight, cotangent)


def sum_kernel(mixed, grad, total, term, paired, half, pieces, chunk, whole, pair_sems, out_sems, in_sems):
    chips = half.shape[0]
    grp, dom = lax.axis_index("grp"), lax.axis_index("dom")
    core = dom % 2
    chip = grp * 8 + dom // 2
    mesh_ids = pl.DeviceIdType.MESH
    partner = {"grp": grp, "dom": dom + 1 - 2 * core}

    def ahead(offset):
        x_hi, y = lax.rem(grp // 4 + offset // 32, 2), lax.rem(grp % 4 + (offset // 8) % 4, 4)
        z, x_lo = lax.rem(dom // 4 + (offset // 2) % 4, 4), lax.rem((dom // 2) % 2 + offset % 2, 2)
        return {"grp": x_hi * 4 + y, "dom": z * 4 + x_lo * 2 + core}

    barrier = pltpu.get_barrier_semaphore()
    pl.semaphore_signal(barrier, inc=1, device_id=partner, device_id_type=mesh_ids)

    @pl.loop(1, chips)
    def _(offset):
        pl.semaphore_signal(barrier, inc=1, device_id=ahead(offset), device_id_type=mesh_ids)

    def own_term(side):
        return lax.dot_general(
            mixed[...], grad[side], (((0,), (0,)), ((), ())), preferred_element_type=jnp.float32
        ).reshape(half.shape)

    term[...] = own_term(1 - core).astype(term.dtype)
    pl.semaphore_wait(barrier, chips)

    swap = pltpu.make_async_remote_copy(
        src_ref=term, dst_ref=paired, send_sem=pair_sems.at[0], recv_sem=pair_sems.at[1],
        device_id=partner, device_id_type=mesh_ids,
    )
    swap.start()
    kept = own_term(core)
    swap.wait()
    half[...] = (kept + paired[...].astype(jnp.float32)).astype(half.dtype)

    def place(offset):
        to = ahead(offset)
        return to["grp"] * 8 + to["dom"] // 2

    @pl.loop(1, chips)
    def _(offset):
        pltpu.make_async_remote_copy(
            src_ref=half.at[place(offset)], dst_ref=pieces.at[offset - 1],
            send_sem=out_sems.at[0], recv_sem=in_sems.at[0],
            device_id=ahead(offset), device_id_type=mesh_ids,
        ).start()

    def all_pieces(number):
        return pltpu.make_async_remote_copy(
            src_ref=pieces, dst_ref=pieces, send_sem=out_sems.at[number], recv_sem=in_sems.at[number],
            device_id=partner, device_id_type=mesh_ids,
        )

    all_pieces(0).wait_recv()
    summed = half[chip].astype(jnp.float32) + jnp.sum(pieces[...].astype(jnp.float32), axis=0)
    chunk[...] = summed.astype(chunk.dtype)
    all_pieces(0).wait_send()

    @pl.loop(1, chips)
    def _(offset):
        pltpu.make_async_remote_copy(
            src_ref=chunk, dst_ref=whole.at[core, chip],
            send_sem=out_sems.at[1], recv_sem=in_sems.at[1],
            device_id=ahead(offset), device_id_type=mesh_ids,
        ).start()

    whole[core, chip] = chunk[...]
    all_pieces(1).wait_recv()
    give = pltpu.make_async_remote_copy(
        src_ref=whole.at[core], dst_ref=whole.at[core], send_sem=pair_sems.at[2], recv_sem=pair_sems.at[3],
        device_id=partner, device_id_type=mesh_ids,
    )
    give.start()
    give.wait()
    columns = whole.shape[3]
    for side in range(2):
        total[:, :, side * columns:(side + 1) * columns] = whole[side]
    all_pieces(1).wait_send()


def sum_terms(mixed, grad):
    chips = lax.axis_size("grp") * lax.axis_size("dom") // 2
    width_in, columns = mixed.shape[1], grad.shape[2]
    share = width_in // chips
    shape = (2, chips, share, columns)
    vmem = pl.BlockSpec(memory_space=pltpu.VMEM)
    whole = pl.pallas_call(
        sum_kernel,
        out_shape=jax.ShapeDtypeStruct((chips, share, 2 * columns), grad.dtype),
        in_specs=[vmem, vmem],
        out_specs=vmem,
        scratch_shapes=[
            pltpu.VMEM(shape[1:], grad.dtype),
            pltpu.VMEM(shape[1:], grad.dtype),
            pltpu.VMEM(shape[1:], grad.dtype),
            pltpu.VMEM((chips - 1, share, columns), grad.dtype),
            pltpu.VMEM((share, columns), grad.dtype),
            pltpu.VMEM(shape, grad.dtype),
            pltpu.SemaphoreType.DMA((4,)),
            pltpu.SemaphoreType.DMA((2,)),
            pltpu.SemaphoreType.DMA((2,)),
        ],
        compiler_params=pltpu.CompilerParams(collective_id=1, has_side_effects=True),
        name="sum_terms",
    )(mixed, grad)
    return whole.reshape(width_in, 2 * columns).astype(jnp.float32)


def shards(features, node_order, block_cols, block_count, block_vals, weight, cotangent):
    arrived, slot = regroup(features, node_order)
    everyone = gather_group(arrived, slot)
    hidden, mixed, grad = local_pass(everyone, block_cols, block_count, block_vals, weight, cotangent)
    return (hidden, sum_terms(mixed, grad))


def solution(mesh):
    placed = (
        P(AXES, None),
        P(AXES),
        P(AXES, None),
        P(AXES),
        P(AXES, None, None, None),
        P(),
        P(AXES, None),
    )
    return jax.shard_map(
        shards,
        mesh=mesh,
        in_specs=placed,
        out_specs=(P(AXES, None), P()),
        check_vma=False,
    )
```

```python
import jax
import jax.numpy as jnp
from jax import lax
from jax.experimental import pallas as pl
from jax.experimental.pallas import tpu as pltpu
from jax.sharding import PartitionSpec as P

AXES = ("grp", "dom")


def order_kernel(order, asked, orders, keep_sem, out_sems, in_sems):
    group, groups, _, rows = orders.shape
    grp, dom = lax.axis_index("grp"), lax.axis_index("dom")
    mesh_ids = pl.DeviceIdType.MESH

    def across(offset):
        x_hi, y = lax.rem(grp // 4 + offset // 4, 2), lax.rem(grp % 4 + offset % 4, 4)
        return {"grp": x_hi * 4 + y, "dom": dom}

    def along(offset):
        z, x_lo = lax.rem(dom // 4 + offset // 4, 4), lax.rem((dom // 2) % 2 + (offset // 2) % 2, 2)
        return {"grp": grp, "dom": z * 4 + x_lo * 2 + lax.rem(dom % 2 + offset % 2, 2)}

    barrier = pltpu.get_barrier_semaphore()
    for offset in range(1, groups):
        pl.semaphore_signal(barrier, inc=1, device_id=across(offset), device_id_type=mesh_ids)
    for offset in range(1, group):
        pl.semaphore_signal(barrier, inc=1, device_id=along(offset), device_id_type=mesh_ids)
    keep = pltpu.make_async_copy(order, orders.at[dom, grp], keep_sem)
    keep.start()
    pl.semaphore_wait(barrier, groups + group - 2)

    for offset in range(1, groups):
        pltpu.make_async_remote_copy(
            src_ref=order, dst_ref=orders.at[dom, grp], send_sem=out_sems.at[0], recv_sem=in_sems.at[0],
            device_id=across(offset), device_id_type=mesh_ids,
        ).start()
    keep.wait()
    some = orders.at[0, pl.ds(0, groups - 1)]
    first = pltpu.make_async_remote_copy(
        src_ref=some, dst_ref=some, send_sem=out_sems.at[0], recv_sem=in_sems.at[0],
        device_id=across(1), device_id_type=mesh_ids,
    )
    first.wait_recv()
    for offset in range(1, group):
        pltpu.make_async_remote_copy(
            src_ref=orders.at[dom], dst_ref=orders.at[dom], send_sem=out_sems.at[1], recv_sem=in_sems.at[1],
            device_id=along(offset), device_id_type=mesh_ids,
        ).start()
    others = orders.at[pl.ds(0, group - 1)]
    every = pltpu.make_async_remote_copy(
        src_ref=others, dst_ref=others, send_sem=out_sems.at[1], recv_sem=in_sems.at[1],
        device_id=along(1), device_id_type=mesh_ids,
    )
    every.wait_recv()
    row = jnp.concatenate([orders[:, number].reshape(group, rows) for number in range(groups)], axis=0)
    row = row - (grp * group + dom) * rows
    mine = jnp.logical_and(row >= 0, row < rows)
    earlier = lax.broadcasted_iota(jnp.int32, (rows, rows), 0) <= lax.broadcasted_iota(jnp.int32, (rows, rows), 1)
    rank = jnp.dot(
        jnp.where(mine, 1.0, 0.0).astype(jnp.bfloat16),
        jnp.where(earlier, 1.0, 0.0).astype(jnp.bfloat16),
        preferred_element_type=jnp.float32,
    )
    rank = jnp.where(mine, rank, 0.0)
    lane = lax.broadcasted_iota(jnp.int32, asked.shape, 1)
    table = jnp.zeros(asked.shape, jnp.float32)
    for number in range(rows // (groups * group)):
        picked = jnp.where(rank == number + 1.0, row.astype(jnp.float32), 0.0)
        table = jnp.where(lane == number, jnp.sum(picked, axis=1, keepdims=True), table)
    asked[...] = table.astype(jnp.int32)
    first.wait_send()
    every.wait_send()


def ask(node_order):
    devices = lax.axis_size("grp") * lax.axis_size("dom")
    rows = node_order.shape[0]
    vmem = pl.BlockSpec(memory_space=pltpu.VMEM)
    return pl.pallas_call(
        order_kernel,
        out_shape=jax.ShapeDtypeStruct((devices, 128), jnp.int32),
        in_specs=[vmem],
        out_specs=vmem,
        scratch_shapes=[
            pltpu.VMEM((lax.axis_size("dom"), lax.axis_size("grp"), 1, rows), jnp.int32),
            pltpu.SemaphoreType.DMA,
            pltpu.SemaphoreType.DMA((2,)),
            pltpu.SemaphoreType.DMA((2,)),
        ],
        compiler_params=pltpu.CompilerParams(collective_id=2, has_side_effects=True),
        name="ask",
    )(node_order.reshape(1, rows))


def regroup(features, node_order):
    row_count, width_in = features.shape
    devices = lax.axis_size("grp") * lax.axis_size("dom")
    per_pair = row_count // devices
    asked_rows = ask(node_order)[:, :per_pair]
    outgoing = features[asked_rows.reshape(-1)].reshape(devices, per_pair, width_in)
    arrived = lax.all_to_all(outgoing, AXES, split_axis=0, concat_axis=0, tiled=True)
    arrived = arrived.reshape(row_count, width_in)
    source = node_order // row_count
    position = jnp.arange(row_count, dtype=jnp.int32)
    before = jnp.logical_and(source[:, None] == source[None, :], position[None, :] < position[:, None])
    slot = source * per_pair + jnp.sum(before.astype(jnp.int32), axis=1)
    return arrived, slot


def piece_plan(rows):
    half = rows // 2
    cut = rows * 11 // 32
    upper = rows - cut
    up = [
        (0, -1, 0, half, None), (0, -1, half, rows, None), (0, 2, 0, half, ("up", 0)),
        (1, -1, 0, cut, ("side", 0)), (1, 2, cut, half, ("side", 2)), (1, 2, 0, cut, ("up", 3)),
    ]
    down = [
        (0, 1, half, rows, None), (0, 1, 0, half, None), (0, 2, half, rows, ("down", 0)),
        (1, 1, upper, rows, ("side", 1)), (1, 2, half, upper, ("side", 3)), (1, 2, upper, rows, ("down", 3)),
    ]
    side = [
        (1, 0, 0, half, None), (1, 0, half, rows, None), (1, -1, cut, half, ("up", 0)),
        (1, 1, half, upper, ("down", 0)), (1, -1, half, rows, ("up", 1)), (1, 1, 0, half, ("down", 1)),
    ]
    return {"up": up, "down": down, "side": side}


ARRIVALS = (
    ("up", 0), ("down", 0), ("side", 0), ("up", 1), ("down", 1), ("side", 1), ("side", 2), ("side", 3),
    ("up", 2), ("down", 2), ("side", 4), ("up", 3), ("down", 3), ("up", 4), ("down", 4), ("side", 5),
    ("up", 5), ("down", 5),
)
LINKS = ("up", "down", "side")


def gather_kernel(arrived, slot, out, own, send_sems, recv_sems, pass_send, pass_recv, keep_sem):
    rows = own.shape[0]
    me = lax.axis_index("dom")
    depth, column, core = me // 4, (me // 2) % 2, me % 2

    def place(other_column, shift, which_core):
        z = lax.rem(depth + shift + 4, 4)
        x = column + other_column * (1 - 2 * column)
        return z * 4 + x * 2 + which_core

    partner = place(0, 0, 1 - core)
    targets = {"up": place(0, 1, core), "down": place(0, -1, core), "side": place(1, 0, core)}

    barrier = pltpu.get_barrier_semaphore()
    for target in (*targets.values(), partner):
        pl.semaphore_signal(barrier, inc=1, device_id={"dom": target}, device_id_type=pl.DeviceIdType.MESH)
    taken = lax.broadcasted_iota(jnp.int32, (rows, rows), 0) == slot[...]
    own[...] = lax.dot_general(
        jnp.where(taken, 1.0, 0.0).astype(own.dtype), arrived[...],
        (((0,), (0,)), ((), ())), preferred_element_type=jnp.float32,
    ).astype(own.dtype)
    keep = pltpu.make_async_copy(own, out.at[me], keep_sem)
    keep.start()
    pl.semaphore_wait(barrier, 4)

    plan = piece_plan(rows)
    moved = {"up": (0, 1), "down": (0, -1), "side": (1, 0)}

    def send(link, number):
        other, shift, low, high, _ = plan[link][number]
        jump, step = moved[link]
        span = pl.ds(low, high - low)
        source_other, source_shift = (other + jump) % 2, shift + step
        owner = place(source_other, source_shift, core)
        slot = LINKS.index(link) * 6 + number
        block = own.at[span] if plan[link][number][4] is None else out.at[owner, span]
        return pltpu.make_async_remote_copy(
            src_ref=block, dst_ref=out.at[owner, span],
            send_sem=send_sems.at[slot], recv_sem=recv_sems.at[slot],
            device_id={"dom": targets[link]}, device_id_type=pl.DeviceIdType.MESH,
        )

    def landed(link, number):
        other, shift, low, high, _ = plan[link][number]
        span = pl.ds(low, high - low)
        slot = LINKS.index(link) * 6 + number
        here = out.at[place(other, shift, core), span]
        return pltpu.make_async_remote_copy(
            src_ref=here, dst_ref=here,
            send_sem=send_sems.at[slot], recv_sem=recv_sems.at[slot],
            device_id={"dom": targets[link]}, device_id_type=pl.DeviceIdType.MESH,
        )

    def hand_over(number, block, there):
        return pltpu.make_async_remote_copy(
            src_ref=block, dst_ref=there,
            send_sem=pass_send.at[number], recv_sem=pass_recv.at[number],
            device_id={"dom": partner}, device_id_type=pl.DeviceIdType.MESH,
        )

    sent = []
    for number in range(2):
        for link in LINKS:
            copy = send(link, number)
            copy.start()
            sent.append(copy)
    copy = hand_over(18, own, out.at[me])
    copy.start()
    sent.append(copy)

    for order, (link, number) in enumerate(ARRIVALS):
        landed(link, number).wait_recv()
        for onward in LINKS:
            for later in range(2, 6):
                if plan[onward][later][4] == (link, number):
                    copy = send(onward, later)
                    copy.start()
                    sent.append(copy)
        other, shift, low, high, _ = plan[link][number]
        here = out.at[place(other, shift, core), pl.ds(low, high - low)]
        copy = hand_over(order, here, here)
        copy.start()
        sent.append(copy)

    hand_over(18, own, out.at[partner]).wait_recv()
    for order, (link, number) in enumerate(ARRIVALS):
        other, shift, low, high, _ = plan[link][number]
        there = out.at[place(other, shift, 1 - core), pl.ds(low, high - low)]
        hand_over(order, there, there).wait_recv()
    for copy in sent:
        copy.wait_send()
    keep.wait()


def gather_group(arrived, slot):
    rows, width_in = arrived.shape
    vmem = pl.BlockSpec(memory_space=pltpu.VMEM)
    group = lax.axis_size("dom")
    return pl.pallas_call(
        gather_kernel,
        out_shape=jax.ShapeDtypeStruct((group, rows, width_in), arrived.dtype),
        in_specs=[vmem, vmem],
        out_specs=pl.BlockSpec(memory_space=pl.ANY),
        scratch_shapes=[
            pltpu.VMEM((rows, width_in), arrived.dtype),
            pltpu.SemaphoreType.DMA((18,)),
            pltpu.SemaphoreType.DMA((18,)),
            pltpu.SemaphoreType.DMA((19,)),
            pltpu.SemaphoreType.DMA((19,)),
            pltpu.SemaphoreType.DMA,
        ],
        compiler_params=pltpu.CompilerParams(collective_id=0, has_side_effects=True),
        name="gather_group",
    )(arrived, slot.reshape(1, rows))


def local_kernel(cols, count, panel, vals, weight, cot, hidden, mixed, grad, chosen, acc, sems):
    tiles, blocks, size, _ = vals.shape

    def fetch(t, k):
        return pltpu.make_async_copy(panel.at[cols[t, k]], chosen.at[t, k], sems.at[t, k])

    def pairs(t):
        return (count[t] + 1) // 2

    def product(t, pair):
        k = 2 * pair
        fetch(t, k).wait()
        fetch(t, k + 1).wait()
        second = vals[t, k + 1]
        second = jnp.where(k + 1 < count[t], second, jnp.zeros_like(second))
        left = jnp.concatenate([vals[t, k], second], axis=1)
        right = chosen[t, pl.ds(k, 2)].reshape(2 * size, chosen.shape[3])
        return jnp.dot(left, right, preferred_element_type=jnp.float32)

    for t in range(tiles):
        @pl.loop(0, 2 * pairs(t))
        def _(k):
            fetch(t, k).start()

    for t in range(tiles):
        acc[...] = product(t, 0)

        @pl.loop(1, pairs(t))
        def _(pair):
            acc[...] += product(t, pair)

        mixed[pl.ds(t * size, size), :] = acc[...].astype(jnp.bfloat16)

    aggregate = jnp.dot(mixed[...], weight[...], preferred_element_type=jnp.float32)
    sig = jax.nn.sigmoid(aggregate)
    hidden[...] = (aggregate * sig).astype(hidden.dtype)
    slope = sig * (1.0 + aggregate * (1.0 - sig))
    grad_agg = (cot[...].astype(jnp.float32) * slope).astype(grad.dtype)
    columns = grad.shape[2]
    for side in range(2):
        grad[side] = grad_agg[:, side * columns:(side + 1) * columns]


def local_pass(everyone, block_cols, block_count, block_vals, weight, cotangent):
    tiles, blocks, size, _ = block_vals.shape
    rows, hidden_units = cotangent.shape
    width_in = weight.shape[0]
    panel = everyone.reshape(-1, size, width_in)
    vmem = pl.BlockSpec(memory_space=pltpu.VMEM)
    smem = pl.BlockSpec(memory_space=pltpu.SMEM)
    return pl.pallas_call(
        local_kernel,
        out_shape=(
            jax.ShapeDtypeStruct((rows, hidden_units), jnp.bfloat16),
            jax.ShapeDtypeStruct((rows, width_in), jnp.bfloat16),
            jax.ShapeDtypeStruct((2, rows, hidden_units // 2), jnp.bfloat16),
        ),
        in_specs=[smem, smem, pl.BlockSpec(memory_space=pl.ANY), vmem, vmem, vmem],
        out_specs=(vmem, vmem, vmem),
        scratch_shapes=[
            pltpu.VMEM((tiles, blocks, size, width_in), jnp.bfloat16),
            pltpu.VMEM((size, width_in), jnp.float32),
            pltpu.SemaphoreType.DMA((tiles, blocks)),
        ],
        name="local_pass",
    )(block_cols, block_count, panel, block_vals, weight, cotangent)


def sum_kernel(mixed, grad, total, term, kept, paired, half, pieces, chunk, whole, pair_sems, out_sems, in_sems):
    chips = half.shape[0]
    grp, dom = lax.axis_index("grp"), lax.axis_index("dom")
    core = dom % 2
    chip = grp * 8 + dom // 2
    mesh_ids = pl.DeviceIdType.MESH
    partner = {"grp": grp, "dom": dom + 1 - 2 * core}

    def ahead(offset):
        x_hi, y = lax.rem(grp // 4 + offset // 32, 2), lax.rem(grp % 4 + (offset // 8) % 4, 4)
        z, x_lo = lax.rem(dom // 4 + (offset // 2) % 4, 4), lax.rem((dom // 2) % 2 + offset % 2, 2)
        return {"grp": x_hi * 4 + y, "dom": z * 4 + x_lo * 2 + core}

    barrier = pltpu.get_barrier_semaphore()
    pl.semaphore_signal(barrier, inc=1, device_id=partner, device_id_type=mesh_ids)

    @pl.loop(1, chips)
    def _(offset):
        pl.semaphore_signal(barrier, inc=1, device_id=ahead(offset), device_id_type=mesh_ids)

    def own_term(side):
        return lax.dot_general(
            mixed[...], grad[side], (((0,), (0,)), ((), ())), preferred_element_type=jnp.float32
        ).reshape(half.shape)

    term[...] = own_term(1 - core).astype(term.dtype)
    pl.semaphore_wait(barrier, chips)

    mid = chips // 2
    near = (grp // 4) * mid
    starts = (mid - near, near)
    spans = tuple(pl.ds(start, mid) for start in starts)
    offsets = ((mid, chips), (1, mid))

    def swap(number):
        return pltpu.make_async_remote_copy(
            src_ref=term.at[spans[number]], dst_ref=paired.at[spans[number]],
            send_sem=pair_sems.at[number], recv_sem=pair_sems.at[2 + number],
            device_id=partner, device_id_type=mesh_ids,
        )

    swap(0).start()
    swap(1).start()
    kept[...] = own_term(core)

    def place(offset):
        to = ahead(offset)
        return to["grp"] * 8 + to["dom"] // 2

    def arriving(number, stage):
        low, high = offsets[number]
        some = pieces.at[pl.ds(low - 1, high - low)]
        return pltpu.make_async_remote_copy(
            src_ref=some, dst_ref=some,
            send_sem=out_sems.at[2 * stage + number], recv_sem=in_sems.at[2 * stage + number],
            device_id=partner, device_id_type=mesh_ids,
        )

    for number in range(2):
        span = spans[number]
        swap(number).wait_recv()
        half[span] = (kept[span] + paired[span].astype(jnp.float32)).astype(half.dtype)

        @pl.loop(*offsets[number])
        def _(offset):
            pltpu.make_async_remote_copy(
                src_ref=half.at[place(offset)], dst_ref=pieces.at[offset - 1],
                send_sem=out_sems.at[number], recv_sem=in_sems.at[number],
                device_id=ahead(offset), device_id_type=mesh_ids,
            ).start()

    summed = half[chip].astype(jnp.float32)
    for number in range(2):
        low, high = offsets[number]
        arriving(number, 0).wait_recv()
        summed = summed + jnp.sum(pieces[pl.ds(low - 1, high - low)].astype(jnp.float32), axis=0)
    chunk[...] = summed.astype(chunk.dtype)

    for number in range(2):
        @pl.loop(*offsets[number])
        def _(offset):
            pltpu.make_async_remote_copy(
                src_ref=chunk, dst_ref=whole.at[core, chip],
                send_sem=out_sems.at[2 + number], recv_sem=in_sems.at[2 + number],
                device_id=ahead(offset), device_id_type=mesh_ids,
            ).start()

    whole[core, chip] = chunk[...]

    def give(number):
        part = whole.at[core, spans[number]]
        return pltpu.make_async_remote_copy(
            src_ref=part, dst_ref=part,
            send_sem=pair_sems.at[4 + number], recv_sem=pair_sems.at[6 + number],
            device_id=partner, device_id_type=mesh_ids,
        )

    for number in range(2):
        arriving(number, 1).wait_recv()
        give(number).start()
    for number in range(2):
        swap(number).wait_send()
        give(number).wait()
        for stage in range(2):
            arriving(number, stage).wait_send()
    columns = whole.shape[3]
    for side in range(2):
        total[:, :, side * columns:(side + 1) * columns] = whole[side]


def sum_terms(mixed, grad):
    chips = lax.axis_size("grp") * lax.axis_size("dom") // 2
    width_in, columns = mixed.shape[1], grad.shape[2]
    share = width_in // chips
    shape = (2, chips, share, columns)
    vmem = pl.BlockSpec(memory_space=pltpu.VMEM)
    whole = pl.pallas_call(
        sum_kernel,
        out_shape=jax.ShapeDtypeStruct((chips, share, 2 * columns), grad.dtype),
        in_specs=[vmem, vmem],
        out_specs=vmem,
        scratch_shapes=[
            pltpu.VMEM(shape[1:], grad.dtype),
            pltpu.VMEM(shape[1:], jnp.float32),
            pltpu.VMEM(shape[1:], grad.dtype),
            pltpu.VMEM(shape[1:], grad.dtype),
            pltpu.VMEM((chips - 1, share, columns), grad.dtype),
            pltpu.VMEM((share, columns), grad.dtype),
            pltpu.VMEM(shape, grad.dtype),
            pltpu.SemaphoreType.DMA((8,)),
            pltpu.SemaphoreType.DMA((4,)),
            pltpu.SemaphoreType.DMA((4,)),
        ],
        compiler_params=pltpu.CompilerParams(collective_id=1, has_side_effects=True),
        name="sum_terms",
    )(mixed, grad)
    return whole.reshape(width_in, 2 * columns).astype(jnp.float32)


def shards(features, node_order, block_cols, block_count, block_vals, weight, cotangent):
    arrived, slot = regroup(features, node_order)
    everyone = gather_group(arrived, slot)
    hidden, mixed, grad = local_pass(everyone, block_cols, block_count, block_vals, weight, cotangent)
    return (hidden, sum_terms(mixed, grad))


def solution(mesh):
    placed = (
        P(AXES, None),
        P(AXES),
        P(AXES, None),
        P(AXES),
        P(AXES, None, None, None),
        P(),
        P(AXES, None),
    )
    return jax.shard_map(
        shards,
        mesh=mesh,
        in_specs=placed,
        out_specs=(P(AXES, None), P()),
        check_vma=False,
    )
```

```python
import jax
import jax.numpy as jnp
from jax import lax
from jax.experimental import pallas as pl
from jax.experimental.pallas import tpu as pltpu
from jax.sharding import PartitionSpec as P

AXES = ("grp", "dom")


def order_kernel(order, asked, orders, keep_sem, out_sems, in_sems):
    group, groups, _, rows = orders.shape
    grp, dom = lax.axis_index("grp"), lax.axis_index("dom")
    mesh_ids = pl.DeviceIdType.MESH

    def across(offset):
        x_hi, y = lax.rem(grp // 4 + offset // 4, 2), lax.rem(grp % 4 + offset % 4, 4)
        return {"grp": x_hi * 4 + y, "dom": dom}

    def along(offset):
        z, x_lo = lax.rem(dom // 4 + offset // 4, 4), lax.rem((dom // 2) % 2 + (offset // 2) % 2, 2)
        return {"grp": grp, "dom": z * 4 + x_lo * 2 + lax.rem(dom % 2 + offset % 2, 2)}

    barrier = pltpu.get_barrier_semaphore()
    for offset in range(1, groups):
        pl.semaphore_signal(barrier, inc=1, device_id=across(offset), device_id_type=mesh_ids)
    for offset in range(1, group):
        pl.semaphore_signal(barrier, inc=1, device_id=along(offset), device_id_type=mesh_ids)
    keep = pltpu.make_async_copy(order, orders.at[dom, grp], keep_sem)
    keep.start()
    pl.semaphore_wait(barrier, groups + group - 2)

    for offset in range(1, groups):
        pltpu.make_async_remote_copy(
            src_ref=order, dst_ref=orders.at[dom, grp], send_sem=out_sems.at[0], recv_sem=in_sems.at[0],
            device_id=across(offset), device_id_type=mesh_ids,
        ).start()
    keep.wait()
    some = orders.at[0, pl.ds(0, groups - 1)]
    first = pltpu.make_async_remote_copy(
        src_ref=some, dst_ref=some, send_sem=out_sems.at[0], recv_sem=in_sems.at[0],
        device_id=across(1), device_id_type=mesh_ids,
    )
    first.wait_recv()
    for offset in range(1, group):
        pltpu.make_async_remote_copy(
            src_ref=orders.at[dom], dst_ref=orders.at[dom], send_sem=out_sems.at[1], recv_sem=in_sems.at[1],
            device_id=along(offset), device_id_type=mesh_ids,
        ).start()
    others = orders.at[pl.ds(0, group - 1)]
    every = pltpu.make_async_remote_copy(
        src_ref=others, dst_ref=others, send_sem=out_sems.at[1], recv_sem=in_sems.at[1],
        device_id=along(1), device_id_type=mesh_ids,
    )
    every.wait_recv()
    row = jnp.concatenate([orders[:, number].reshape(group, rows) for number in range(groups)], axis=0)
    row = row - (grp * group + dom) * rows
    mine = jnp.logical_and(row >= 0, row < rows)
    earlier = lax.broadcasted_iota(jnp.int32, (rows, rows), 0) <= lax.broadcasted_iota(jnp.int32, (rows, rows), 1)
    rank = jnp.dot(
        jnp.where(mine, 1.0, 0.0).astype(jnp.bfloat16),
        jnp.where(earlier, 1.0, 0.0).astype(jnp.bfloat16),
        preferred_element_type=jnp.float32,
    )
    rank = jnp.where(mine, rank, 0.0)
    lane = lax.broadcasted_iota(jnp.int32, asked.shape, 1)
    table = jnp.zeros(asked.shape, jnp.float32)
    for number in range(rows // (groups * group)):
        picked = jnp.where(rank == number + 1.0, row.astype(jnp.float32), 0.0)
        table = jnp.where(lane == number, jnp.sum(picked, axis=1, keepdims=True), table)
    asked[...] = table.astype(jnp.int32)
    first.wait_send()
    every.wait_send()


def ask(node_order):
    devices = lax.axis_size("grp") * lax.axis_size("dom")
    rows = node_order.shape[0]
    vmem = pl.BlockSpec(memory_space=pltpu.VMEM)
    return pl.pallas_call(
        order_kernel,
        out_shape=jax.ShapeDtypeStruct((devices, 128), jnp.int32),
        in_specs=[vmem],
        out_specs=vmem,
        scratch_shapes=[
            pltpu.VMEM((lax.axis_size("dom"), lax.axis_size("grp"), 1, rows), jnp.int32),
            pltpu.SemaphoreType.DMA,
            pltpu.SemaphoreType.DMA((2,)),
            pltpu.SemaphoreType.DMA((2,)),
        ],
        compiler_params=pltpu.CompilerParams(collective_id=2, has_side_effects=True),
        name="ask",
    )(node_order.reshape(1, rows))


def regroup(features, node_order):
    row_count, width_in = features.shape
    devices = lax.axis_size("grp") * lax.axis_size("dom")
    per_pair = row_count // devices
    asked_rows = ask(node_order)[:, :per_pair]
    outgoing = features[asked_rows.reshape(-1)].reshape(devices, per_pair, width_in)
    arrived = lax.all_to_all(outgoing, AXES, split_axis=0, concat_axis=0, tiled=True)
    arrived = arrived.reshape(row_count, width_in)
    source = node_order // row_count
    position = jnp.arange(row_count, dtype=jnp.int32)
    before = jnp.logical_and(source[:, None] == source[None, :], position[None, :] < position[:, None])
    slot = source * per_pair + jnp.sum(before.astype(jnp.int32), axis=1)
    return arrived, slot


def piece_plan(rows):
    half = rows // 2
    cut = rows * 11 // 32
    upper = rows - cut
    up = [
        (0, -1, 0, half, None), (0, -1, half, rows, None), (0, 2, 0, half, ("up", 0)),
        (1, -1, 0, cut, ("side", 0)), (1, 2, cut, half, ("side", 2)), (1, 2, 0, cut, ("up", 3)),
    ]
    down = [
        (0, 1, half, rows, None), (0, 1, 0, half, None), (0, 2, half, rows, ("down", 0)),
        (1, 1, upper, rows, ("side", 1)), (1, 2, half, upper, ("side", 3)), (1, 2, upper, rows, ("down", 3)),
    ]
    side = [
        (1, 0, 0, half, None), (1, 0, half, rows, None), (1, -1, cut, half, ("up", 0)),
        (1, 1, half, upper, ("down", 0)), (1, -1, half, rows, ("up", 1)), (1, 1, 0, half, ("down", 1)),
    ]
    return {"up": up, "down": down, "side": side}


ARRIVALS = (
    ("up", 0), ("down", 0), ("side", 0), ("up", 1), ("down", 1), ("side", 1), ("side", 2), ("side", 3),
    ("up", 2), ("down", 2), ("side", 4), ("up", 3), ("down", 3), ("up", 4), ("down", 4), ("side", 5),
    ("up", 5), ("down", 5),
)
LINKS = ("up", "down", "side")


def gather_kernel(arrived, slot, out, own, send_sems, recv_sems, pass_send, pass_recv, keep_sem):
    rows = own.shape[0]
    me = lax.axis_index("dom")
    depth, column, core = me // 4, (me // 2) % 2, me % 2

    def place(other_column, shift, which_core):
        z = lax.rem(depth + shift + 4, 4)
        x = column + other_column * (1 - 2 * column)
        return z * 4 + x * 2 + which_core

    partner = place(0, 0, 1 - core)
    targets = {"up": place(0, 1, core), "down": place(0, -1, core), "side": place(1, 0, core)}

    barrier = pltpu.get_barrier_semaphore()
    for target in (*targets.values(), partner):
        pl.semaphore_signal(barrier, inc=1, device_id={"dom": target}, device_id_type=pl.DeviceIdType.MESH)
    taken = lax.broadcasted_iota(jnp.int32, (rows, rows), 0) == slot[...]
    own[...] = lax.dot_general(
        jnp.where(taken, 1.0, 0.0).astype(own.dtype), arrived[...],
        (((0,), (0,)), ((), ())), preferred_element_type=jnp.float32,
    ).astype(own.dtype)
    keep = pltpu.make_async_copy(own, out.at[me], keep_sem)
    keep.start()
    pl.semaphore_wait(barrier, 4)

    plan = piece_plan(rows)
    moved = {"up": (0, 1), "down": (0, -1), "side": (1, 0)}

    def send(link, number):
        other, shift, low, high, _ = plan[link][number]
        jump, step = moved[link]
        span = pl.ds(low, high - low)
        source_other, source_shift = (other + jump) % 2, shift + step
        owner = place(source_other, source_shift, core)
        slot = LINKS.index(link) * 6 + number
        block = own.at[span] if plan[link][number][4] is None else out.at[owner, span]
        return pltpu.make_async_remote_copy(
            src_ref=block, dst_ref=out.at[owner, span],
            send_sem=send_sems.at[slot], recv_sem=recv_sems.at[slot],
            device_id={"dom": targets[link]}, device_id_type=pl.DeviceIdType.MESH,
        )

    def landed(link, number):
        other, shift, low, high, _ = plan[link][number]
        span = pl.ds(low, high - low)
        slot = LINKS.index(link) * 6 + number
        here = out.at[place(other, shift, core), span]
        return pltpu.make_async_remote_copy(
            src_ref=here, dst_ref=here,
            send_sem=send_sems.at[slot], recv_sem=recv_sems.at[slot],
            device_id={"dom": targets[link]}, device_id_type=pl.DeviceIdType.MESH,
        )

    def hand_over(number, block, there):
        return pltpu.make_async_remote_copy(
            src_ref=block, dst_ref=there,
            send_sem=pass_send.at[number], recv_sem=pass_recv.at[number],
            device_id={"dom": partner}, device_id_type=pl.DeviceIdType.MESH,
        )

    sent = []
    for number in range(2):
        for link in LINKS:
            copy = send(link, number)
            copy.start()
            sent.append(copy)
    copy = hand_over(18, own, out.at[me])
    copy.start()
    sent.append(copy)

    for order, (link, number) in enumerate(ARRIVALS):
        landed(link, number).wait_recv()
        for onward in LINKS:
            for later in range(2, 6):
                if plan[onward][later][4] == (link, number):
                    copy = send(onward, later)
                    copy.start()
                    sent.append(copy)
        other, shift, low, high, _ = plan[link][number]
        here = out.at[place(other, shift, core), pl.ds(low, high - low)]
        copy = hand_over(order, here, here)
        copy.start()
        sent.append(copy)

    hand_over(18, own, out.at[partner]).wait_recv()
    for order, (link, number) in enumerate(ARRIVALS):
        other, shift, low, high, _ = plan[link][number]
        there = out.at[place(other, shift, 1 - core), pl.ds(low, high - low)]
        hand_over(order, there, there).wait_recv()
    for copy in sent:
        copy.wait_send()
    keep.wait()


def gather_group(arrived, slot):
    rows, width_in = arrived.shape
    vmem = pl.BlockSpec(memory_space=pltpu.VMEM)
    group = lax.axis_size("dom")
    return pl.pallas_call(
        gather_kernel,
        out_shape=jax.ShapeDtypeStruct((group, rows, width_in), arrived.dtype),
        in_specs=[vmem, vmem],
        out_specs=pl.BlockSpec(memory_space=pl.ANY),
        scratch_shapes=[
            pltpu.VMEM((rows, width_in), arrived.dtype),
            pltpu.SemaphoreType.DMA((18,)),
            pltpu.SemaphoreType.DMA((18,)),
            pltpu.SemaphoreType.DMA((19,)),
            pltpu.SemaphoreType.DMA((19,)),
            pltpu.SemaphoreType.DMA,
        ],
        compiler_params=pltpu.CompilerParams(collective_id=0, has_side_effects=True),
        name="gather_group",
    )(arrived, slot.reshape(1, rows))


def local_kernel(cols, count, panel, vals, weight, cot, hidden, mixed, grad, chosen, acc, sems):
    tiles, blocks, size, _ = vals.shape

    def fetch(t, k):
        return pltpu.make_async_copy(panel.at[cols[t, k]], chosen.at[t, k], sems.at[t, k])

    depth = 4

    def bundles(t):
        return (count[t] + depth - 1) // depth

    def product(t, bundle):
        first = depth * bundle
        parts = []
        for extra in range(depth):
            fetch(t, first + extra).wait()
            part = vals[t, first + extra]
            parts.append(jnp.where(first + extra < count[t], part, jnp.zeros_like(part)))
        right = chosen[t, pl.ds(first, depth)].reshape(depth * size, chosen.shape[3])
        return jnp.dot(jnp.concatenate(parts, axis=1), right, preferred_element_type=jnp.float32)

    for t in range(tiles):
        @pl.loop(0, depth * bundles(t))
        def _(k):
            fetch(t, k).start()

    for t in range(tiles):
        acc[...] = product(t, 0)

        @pl.loop(1, bundles(t))
        def _(bundle):
            acc[...] += product(t, bundle)

        mixed[pl.ds(t * size, size), :] = acc[...].astype(jnp.bfloat16)

    aggregate = jnp.dot(mixed[...], weight[...], preferred_element_type=jnp.float32)
    sig = jax.nn.sigmoid(aggregate)
    hidden[...] = (aggregate * sig).astype(hidden.dtype)
    slope = sig * (1.0 + aggregate * (1.0 - sig))
    grad_agg = (cot[...].astype(jnp.float32) * slope).astype(grad.dtype)
    columns = grad.shape[2]
    for side in range(2):
        grad[side] = grad_agg[:, side * columns:(side + 1) * columns]


def local_pass(everyone, block_cols, block_count, block_vals, weight, cotangent):
    tiles, blocks, size, _ = block_vals.shape
    rows, hidden_units = cotangent.shape
    width_in = weight.shape[0]
    panel = everyone.reshape(-1, size, width_in)
    vmem = pl.BlockSpec(memory_space=pltpu.VMEM)
    smem = pl.BlockSpec(memory_space=pltpu.SMEM)
    return pl.pallas_call(
        local_kernel,
        out_shape=(
            jax.ShapeDtypeStruct((rows, hidden_units), jnp.bfloat16),
            jax.ShapeDtypeStruct((rows, width_in), jnp.bfloat16),
            jax.ShapeDtypeStruct((2, rows, hidden_units // 2), jnp.bfloat16),
        ),
        in_specs=[smem, smem, pl.BlockSpec(memory_space=pl.ANY), vmem, vmem, vmem],
        out_specs=(vmem, vmem, vmem),
        scratch_shapes=[
            pltpu.VMEM((tiles, blocks, size, width_in), jnp.bfloat16),
            pltpu.VMEM((size, width_in), jnp.float32),
            pltpu.SemaphoreType.DMA((tiles, blocks)),
        ],
        name="local_pass",
    )(block_cols, block_count, panel, block_vals, weight, cotangent)


def sum_kernel(mixed, grad, total, term, kept, paired, half, pieces, chunk, whole, pair_sems, out_sems, in_sems):
    chips = half.shape[0]
    grp, dom = lax.axis_index("grp"), lax.axis_index("dom")
    core = dom % 2
    chip = grp * 8 + dom // 2
    mesh_ids = pl.DeviceIdType.MESH
    partner = {"grp": grp, "dom": dom + 1 - 2 * core}

    def ahead(offset):
        x_hi, y = lax.rem(grp // 4 + offset // 32, 2), lax.rem(grp % 4 + (offset // 8) % 4, 4)
        z, x_lo = lax.rem(dom // 4 + (offset // 2) % 4, 4), lax.rem((dom // 2) % 2 + offset % 2, 2)
        return {"grp": x_hi * 4 + y, "dom": z * 4 + x_lo * 2 + core}

    barrier = pltpu.get_barrier_semaphore()
    pl.semaphore_signal(barrier, inc=1, device_id=partner, device_id_type=mesh_ids)

    @pl.loop(1, chips)
    def _(offset):
        pl.semaphore_signal(barrier, inc=1, device_id=ahead(offset), device_id_type=mesh_ids)

    def own_term(side):
        return lax.dot_general(
            mixed[...], grad[side], (((0,), (0,)), ((), ())), preferred_element_type=jnp.float32
        ).reshape(half.shape)

    term[...] = own_term(1 - core).astype(term.dtype)
    pl.semaphore_wait(barrier, chips)

    mid = chips // 2
    near = (grp // 4) * mid
    starts = (mid - near, near)
    spans = tuple(pl.ds(start, mid) for start in starts)
    offsets = ((mid, chips), (1, mid))

    def swap(number):
        return pltpu.make_async_remote_copy(
            src_ref=term.at[spans[number]], dst_ref=paired.at[spans[number]],
            send_sem=pair_sems.at[number], recv_sem=pair_sems.at[2 + number],
            device_id=partner, device_id_type=mesh_ids,
        )

    swap(0).start()
    swap(1).start()
    kept[...] = own_term(core)

    def place(offset):
        to = ahead(offset)
        return to["grp"] * 8 + to["dom"] // 2

    def arriving(number, stage):
        low, high = offsets[number]
        some = pieces.at[pl.ds(low - 1, high - low)]
        return pltpu.make_async_remote_copy(
            src_ref=some, dst_ref=some,
            send_sem=out_sems.at[2 * stage + number], recv_sem=in_sems.at[2 * stage + number],
            device_id=partner, device_id_type=mesh_ids,
        )

    for number in range(2):
        span = spans[number]
        swap(number).wait_recv()
        half[span] = (kept[span] + paired[span].astype(jnp.float32)).astype(half.dtype)

        @pl.loop(*offsets[number])
        def _(offset):
            pltpu.make_async_remote_copy(
                src_ref=half.at[place(offset)], dst_ref=pieces.at[offset - 1],
                send_sem=out_sems.at[number], recv_sem=in_sems.at[number],
                device_id=ahead(offset), device_id_type=mesh_ids,
            ).start()

    summed = half[chip].astype(jnp.float32)
    for number in range(2):
        low, high = offsets[number]
        arriving(number, 0).wait_recv()
        summed = summed + jnp.sum(pieces[pl.ds(low - 1, high - low)].astype(jnp.float32), axis=0)
    chunk[...] = summed.astype(chunk.dtype)

    for number in range(2):
        @pl.loop(*offsets[number])
        def _(offset):
            pltpu.make_async_remote_copy(
                src_ref=chunk, dst_ref=whole.at[core, chip],
                send_sem=out_sems.at[2 + number], recv_sem=in_sems.at[2 + number],
                device_id=ahead(offset), device_id_type=mesh_ids,
            ).start()

    whole[core, chip] = chunk[...]

    def give(number):
        part = whole.at[core, spans[number]]
        return pltpu.make_async_remote_copy(
            src_ref=part, dst_ref=part,
            send_sem=pair_sems.at[4 + number], recv_sem=pair_sems.at[6 + number],
            device_id=partner, device_id_type=mesh_ids,
        )

    for number in range(2):
        arriving(number, 1).wait_recv()
        give(number).start()
    for number in range(2):
        swap(number).wait_send()
        give(number).wait()
        for stage in range(2):
            arriving(number, stage).wait_send()
    columns = whole.shape[3]
    for side in range(2):
        total[:, :, side * columns:(side + 1) * columns] = whole[side]


def sum_terms(mixed, grad):
    chips = lax.axis_size("grp") * lax.axis_size("dom") // 2
    width_in, columns = mixed.shape[1], grad.shape[2]
    share = width_in // chips
    shape = (2, chips, share, columns)
    vmem = pl.BlockSpec(memory_space=pltpu.VMEM)
    whole = pl.pallas_call(
        sum_kernel,
        out_shape=jax.ShapeDtypeStruct((chips, share, 2 * columns), grad.dtype),
        in_specs=[vmem, vmem],
        out_specs=vmem,
        scratch_shapes=[
            pltpu.VMEM(shape[1:], grad.dtype),
            pltpu.VMEM(shape[1:], jnp.float32),
            pltpu.VMEM(shape[1:], grad.dtype),
            pltpu.VMEM(shape[1:], grad.dtype),
            pltpu.VMEM((chips - 1, share, columns), grad.dtype),
            pltpu.VMEM((share, columns), grad.dtype),
            pltpu.VMEM(shape, grad.dtype),
            pltpu.SemaphoreType.DMA((8,)),
            pltpu.SemaphoreType.DMA((4,)),
            pltpu.SemaphoreType.DMA((4,)),
        ],
        compiler_params=pltpu.CompilerParams(collective_id=1, has_side_effects=True),
        name="sum_terms",
    )(mixed, grad)
    return whole.reshape(width_in, 2 * columns).astype(jnp.float32)


def shards(features, node_order, block_cols, block_count, block_vals, weight, cotangent):
    arrived, slot = regroup(features, node_order)
    everyone = gather_group(arrived, slot)
    hidden, mixed, grad = local_pass(everyone, block_cols, block_count, block_vals, weight, cotangent)
    return (hidden, sum_terms(mixed, grad))


def solution(mesh):
    placed = (
        P(AXES, None),
        P(AXES),
        P(AXES, None),
        P(AXES),
        P(AXES, None, None, None),
        P(),
        P(AXES, None),
    )
    return jax.shard_map(
        shards,
        mesh=mesh,
        in_specs=placed,
        out_specs=(P(AXES, None), P()),
        check_vma=False,
    )
```
